32 devices in a mesh: leaf: 16 (over z, y, x), rhs: 2 (over core).
Axes of the slice: x: 2, y: 2, z: 4, core: 2. Of those that a mesh axis runs over, the one named last changes fastest.
Arguments:
- rhs_matrix: float32 [16384, 128], P('leaf', 'rhs'), may hold values from -21 to 21, as said below
- initial_guess: float32 [16384, 128], P('leaf', 'rhs'), may hold values from -4 to 4
- leaf_blocks: float32 [16384, 1024], P(('leaf', 'rhs')), may hold values from -2 to 8, as said below
- row_bases: float32 [4, 96, 16384], P(None, None, 'leaf'), may hold values from -1 to 1
- couplings: float32 [4, 96, 96], replicated, may hold values from -100 to 100, as said below
Outputs:
- solution: float32 [16384, 128], P('leaf', 'rhs')
- residual: float32 [16384, 128], P('leaf', 'rhs')
The draws below stay inside these ranges and needn't reach their ends.
Inputs may be any that keep to these rules, and one draw needn't show every extreme that they name: `rhs_matrix`: column scales may differ; rows grow in scale toward the end of the rows. `leaf_blocks`: every 1024 x 1024 block is symmetric positive definite. `couplings`: every coupling matrix is symmetric positive definite.
All inputs are finite; a program needn't handle non-finite values.
Results may differ from the reference program's by a relative error of at most 0.0003.
Values sent between devices are 32-bit elements; how exact they have to be, the bound alone decides.
A program may use at most 64 MiB of HBM per device.

```python
import jax
import jax.numpy as jnp
from jax import lax

LEAF = 1024
RANK = 96
ITERS = 1
BLOCKS = 16
ROWS = 16384
RHS = 128
LEVELS = 4


def draw_rhs_matrix(key, part):
    first_key = jax.random.fold_in(jax.random.fold_in(key, 11), 0)
    position = jnp.arange(ROWS, dtype=jnp.float32)[:, None] / ROWS
    values = jax.random.truncated_normal(first_key, -4.0, 4.0, (ROWS, RHS), jnp.float32)
    return values * (1.0 + 2.0 * position)


def draw_leaf_blocks(key, part):
    first_key, second_key = jax.random.split(jax.random.fold_in(key, 23))
    raw_values = jax.random.truncated_normal(first_key, -4.0, 4.0, (BLOCKS, LEAF, LEAF), jnp.float32)
    symmetric = (raw_values + jnp.swapaxes(raw_values, 1, 2)) / jnp.sqrt(2.0 * LEAF)
    noise_level = jax.random.uniform(second_key, (BLOCKS, LEAF), jnp.float32, 4.5, 5.5)
    identity = jnp.eye(LEAF, dtype=jnp.float32)
    blocks = symmetric + noise_level[:, :, None] * identity[None, :, :]
    return blocks.reshape(ROWS, LEAF)


def draw_row_bases(key, part):
    raw_values = jax.random.truncated_normal(jax.random.fold_in(key, 37), -4.0, 4.0, (LEVELS, RANK, ROWS), jnp.float32)
    node_rows = LEAF * 2.0 ** (jnp.arange(LEVELS, dtype=jnp.float32) + 1.0)
    return raw_values / jnp.sqrt(node_rows)[:, None, None]


def draw_couplings(key, part):
    raw_values = jax.random.truncated_normal(jax.random.fold_in(key, 41), -4.0, 4.0, (LEVELS, RANK, RANK), jnp.float32)
    gram = jnp.einsum('krs,kqs->krq', raw_values, raw_values, precision=lax.Precision.HIGHEST) / RANK
    gram = 0.5 * (gram + jnp.swapaxes(gram, 1, 2)) + 0.5 * jnp.eye(RANK, dtype=jnp.float32)[None]
    node_rows = LEAF * 2.0 ** (jnp.arange(LEVELS, dtype=jnp.float32) + 1.0)
    strength = 0.3 * jnp.sqrt(node_rows / RANK)
    return gram * strength[:, None, None]


def steps_of(key, shape, pieces, least, largest):
    gain, own = 1.0, jax.random.fold_in(key, 6)
    for dim, parts in pieces:
        draws = jnp.exp(jax.random.uniform(jax.random.fold_in(own, dim), (parts,), jnp.float32, least / len(pieces), largest / len(pieces)))
        gain = gain * jnp.repeat(draws, shape[dim] // parts).reshape([-1 if axis == dim else 1 for axis in range(len(shape))])
    return gain


def noise(own_key, extent, width, bound, cuts=(), held_as=jnp.bfloat16):
    values = width * jax.random.normal(own_key, extent, jnp.float32)
    if cuts:
        values = values * steps_of(own_key, extent, cuts, -0.22, 0.18)
    return jnp.clip(values, -bound, bound).astype(held_as)


def setup_inputs(seed: int = 0) -> dict:
    seeds = jax.random.split(jax.random.key(seed), 6)
    return {
        "rhs_matrix": draw_rhs_matrix(jax.random.fold_in(seeds[5], 71), 0),
        "initial_guess": noise(seeds[1], (ROWS, RHS), 0.3, 4.0, ((0, 16), (1, 2)), jnp.float32),
        "leaf_blocks": draw_leaf_blocks(jax.random.fold_in(seeds[5], 71), 0),
        "row_bases": draw_row_bases(jax.random.fold_in(seeds[5], 71), 0),
        "couplings": draw_couplings(jax.random.fold_in(seeds[5], 71), 0),
    }


PRECISE = lax.Precision.HIGHEST


def apply_kernel(operand, leaf_blocks, row_bases, couplings):
    blocks = leaf_blocks.reshape(BLOCKS, LEAF, LEAF)
    local_cols = operand.reshape(BLOCKS, LEAF, RHS)
    result = jnp.einsum("bij,bjc->bic", blocks, local_cols, precision=PRECISE).reshape(ROWS, RHS)
    for tier_index in range(LEVELS):
        node_count = ROWS // (LEAF * 2 ** (tier_index + 1))
        tier_basis = row_bases[tier_index].reshape(RANK, node_count, -1)
        grouped = operand.reshape(node_count, -1, RHS)
        node_sums = jnp.einsum("rnm,nmc->nrc", tier_basis, grouped, precision=PRECISE)
        coupled = jnp.einsum("rs,nsc->nrc", couplings[tier_index], node_sums, precision=PRECISE)
        spread_back = jnp.einsum("rnm,nrc->nmc", tier_basis, coupled, precision=PRECISE)
        result = result + spread_back.reshape(ROWS, RHS)
    return result


def reference(rhs_matrix, initial_guess, leaf_blocks, row_bases, couplings):
    solution = initial_guess
    residual = rhs_matrix - apply_kernel(initial_guess, leaf_blocks, row_bases, couplings)
    direction = residual
    norm_now = jnp.sum(residual * residual, axis=0)
    for turn_index in range(ITERS):
        kernel_image = apply_kernel(direction, leaf_blocks, row_bases, couplings)
        step_size = norm_now / jnp.sum(direction * kernel_image, axis=0)
        solution = solution + step_size * direction
        residual = residual - step_size * kernel_image
        norm_next = jnp.sum(residual * residual, axis=0)
        direction = residual + (norm_next / norm_now) * direction
        norm_now = norm_next
    return solution, residual
```

```python
import functools

import jax
import jax.numpy as jnp
from jax import lax
from jax.experimental import pallas as pl
from jax.experimental.pallas import tpu as pltpu
from jax.sharding import PartitionSpec as P

MESH = pl.DeviceIdType.MESH
F32 = jnp.float32
BF16 = jnp.bfloat16
LANES = 128
PIECES = 1
NN = (((1,), (0,)), ((), ()))
NT = (((1,), (1,)), ((), ()))


def halves(value):
    high = value.astype(BF16)
    return high, (value - high.astype(F32)).astype(BF16)


def dot3(left, right, dims):
    rows = left[0].shape[0]
    stacked = lax.dot_general(
        jnp.concatenate(left, axis=0), right[0], dims, preferred_element_type=F32
    )
    cross = lax.dot_general(left[0], right[1], dims, preferred_element_type=F32)
    return stacked[:rows] + (stacked[rows:] + cross)


def lane_fold(value):
    total = value[:, :LANES]
    for start in range(LANES, value.shape[1], LANES):
        total = total + value[:, start : start + LANES]
    return total


def kernel(
    x_hbm, b_hbm, d_hbm, u_hbm, c_hbm,
    r_ref, image_ref, step_ref,
    x_v, b_v, d_v, u_v, c_v,
    d_hi, d_lo, u_hi, u_lo, c_hi, c_lo, v_hi, v_lo, cc_hi, cc_lo,
    sums, base, z_in, w_out, w_in, t_out, t_in, s_out, s_in, q_out, q_in,
    local_sem, z_send, z_recv, w_send, w_recv, t_send, t_recv, s_send, s_recv, q_send, q_recv,
):
    tiers, rank, leaf = u_v.shape
    cols = x_v.shape[0]
    half = leaf // 2
    me, core = lax.axis_index("leaf"), lax.axis_index("rhs")
    other = 1 - core
    mine = pl.ds(pl.multiple_of(core * half, half), half)
    theirs = pl.ds(pl.multiple_of(other * half, half), half)

    def flip(leaf_index, stage):
        bit = 2**stage
        return leaf_index + bit * (1 - 2 * ((leaf_index // bit) % 2))

    def peer(stage):
        return (flip(me, stage), core)

    groups = [tuple(range(low, min(low + 2, tiers))) for low in range(0, tiers, 2)]
    group_peers = []
    for bits in groups:
        peers = [peer(stage) for stage in bits]
        if len(bits) == 2:
            peers.append((flip(flip(me, bits[0]), bits[1]), core))
        group_peers.append(peers)

    barrier = pltpu.get_barrier_semaphore()
    steps = groups

    def step_peers(step, tier):
        bits = steps[step]
        if len(bits) == 1 or tier < bits[1]:
            return [peer(bits[0])]
        return group_peers[bits[0] // 2]

    targets = [(me, other)] + [device for peers in group_peers for device in peers]
    for target in targets:
        pl.semaphore_signal(barrier, inc=1, device_id=target, device_id_type=MESH)

    tier_pairs = [slice(max(last - 2, 0), last) for last in range(tiers, 0, -2)]
    arrays = [(x_hbm, x_v)]
    arrays += [(u_hbm.at[pair], u_v.at[pair]) for pair in tier_pairs]
    arrays += [(d_hbm, d_v), (c_hbm, c_v), (b_hbm, b_v)]
    loads = [
        pltpu.make_async_copy(source, target, local_sem.at[index])
        for index, (source, target) in enumerate(arrays)
    ]
    for load in loads:
        load.start()
    x_load, *u_loads, d_load, c_load, b_load = loads

    def remote(source, target, send, recv, device):
        return pltpu.make_async_remote_copy(
            src_ref=source, dst_ref=target, send_sem=send, recv_sem=recv,
            device_id=device, device_id_type=MESH,
        )

    def z_copy(turn):
        source = x_hbm if turn == 0 else r_ref
        return remote(
            source.at[:, theirs], z_in.at[turn], z_send.at[turn], z_recv.at[turn], (me, other)
        )

    def w_copy(turn):
        return remote(
            w_out.at[turn], w_in.at[turn], w_send.at[turn], w_recv.at[turn], (me, other)
        )

    def pieces(tier):
        count = PIECES if tier >= tiers - 2 else 1
        size = cols // count
        return [(index, slice(index * size, (index + 1) * size)) for index in range(count)]

    def t_copy(turn, step, tier, piece, index):
        number, rows = piece
        out, into = (turn, step, tier, rows), (turn, step, tier, index, rows)
        sem = (turn, step, tier, index, number)
        return remote(
            t_out.at[out], t_in.at[into], t_send.at[sem], t_recv.at[sem], step_peers(step, tier)[index]
        )

    def send_tier(turn, step, tier, piece):
        for index in reversed(range(len(step_peers(step, tier)))):
            t_copy(turn, step, tier, piece, index).start()

    def s_copy(group, index):
        at = (group, index)
        return remote(
            s_out.at[group], s_in.at[at], s_send.at[at], s_recv.at[at], group_peers[group][index]
        )

    def q_copy(group):
        return remote(
            q_out.at[group], q_in.at[group], q_send.at[group], q_recv.at[group], group_peers[group][1]
        )

    padded = u_hi.shape[1]
    if padded > rank:
        blank = jnp.zeros((tiers, padded - rank, leaf), BF16)
        u_hi[:, rank:, :] = blank
        u_lo[:, rank:, :] = blank
    c_hi[...] = jnp.zeros_like(c_hi)
    c_lo[...] = jnp.zeros_like(c_lo)

    def project(turn):
        for index, pair in enumerate(tier_pairs):
            first, last = pair.start, pair.stop
            if turn == 0:
                u_loads[index].wait()
                for tier in range(first, last):
                    u_hi[tier, :rank], u_lo[tier, :rank] = halves(u_v[tier])
            bases = tuple(
                part[pair].reshape((last - first) * padded, leaf) for part in (u_hi, u_lo)
            )
            products = dot3((v_hi[...], v_lo[...]), bases, NT)
            for tier in range(first, last):
                start = (tier - first) * padded
                t_out[turn, 0, tier] = products[:, start : start + padded]
            if turn == 0 and index == 0:
                pl.semaphore_wait(barrier, len(targets))
            for tier in range(last - 1, first - 1, -1):
                for piece in pieces(tier):
                    send_tier(turn, 0, tier, piece)
            if turn == 0 and index == 0:
                z_copy(0).start()

    def combine(turn, step, tier):
        parts = []
        for piece in pieces(tier):
            rows = piece[1]
            part = t_out[turn, step, tier, rows]
            for index in range(len(step_peers(step, tier))):
                t_copy(turn, step, tier, piece, index).wait_recv()
                part = part + t_in[turn, step, tier, index, rows]
            if tier > steps[step][-1]:
                t_out[turn, step + 1, tier, rows] = part
                send_tier(turn, step + 1, tier, piece)
            parts.append(part)
        if tier > steps[step][-1]:
            return None
        total = jnp.concatenate(parts, axis=0)
        coupled = dot3(halves(total), (c_hi[tier], c_lo[tier]), NT)
        at = slice(tier * padded, (tier + 1) * padded)
        cc_hi[:, at], cc_lo[:, at] = halves(coupled)
        return lane_fold(total * coupled)

    def spread(first, last):
        at = slice(first * padded, last * padded)
        count = (last - first) * padded
        bases = tuple(part[first:last].reshape(count, leaf) for part in (u_hi, u_lo))
        return dot3((cc_hi[:, at], cc_lo[:, at]), bases, NN)

    def for_partner(turn):
        z_copy(turn).wait_recv()
        block = (d_hi[:, mine], d_lo[:, mine])
        w_out[turn] = dot3(halves(z_in[turn]), block, NT)
        w_copy(turn).start()

    def own_dense():
        sums[:, mine] = dot3((v_hi[...], v_lo[...]), (d_hi[...], d_lo[...]), NT)
        sums[:, theirs] = dot3(
            (v_hi[:, mine], v_lo[:, mine]), (d_hi[:, theirs], d_lo[:, theirs]), NN
        )

    def add_partner(turn):
        w_copy(turn).wait_recv()
        sums[:, theirs] = sums[:, theirs] + w_in[turn]

    x_load.wait()
    v_hi[...], v_lo[...] = halves(x_v[...])
    project(0)
    d_load.wait()
    d_hi[...], d_lo[...] = halves(d_v[...])
    for_partner(0)
    c_load.wait()
    c_hi[:, :rank, :rank], c_lo[:, :rank, :rank] = halves(c_v[...])
    low = steps[-1][0]
    for step, bits in enumerate(steps):
        if step == min(1, len(steps) - 1):
            own_dense()
        if step == len(steps) - 1:
            b_load.wait()
            add_partner(0)
            total = b_v[...] - sums[...]
            if low > 0:
                total = total - spread(0, low)
            base[...] = total
        for tier in range(tiers - 1, bits[0] - 1, -1):
            combine(0, step, tier)
    residual = base[...] - spread(low, tiers)
    r_ref[...] = residual
    z_copy(1).start()
    v_hi[...], v_lo[...] = halves(residual)

    project(1)
    own_dense()
    for_partner(1)

    def row_of(upper, lower):
        stacked = jnp.concatenate([upper, lower], axis=0)
        return jnp.sum(stacked.T, axis=0, keepdims=True)

    def start_sums(group, row):
        s_out[group] = jnp.broadcast_to(row, s_out.shape[1:])
        for index in range(len(group_peers[group])):
            s_copy(group, index).start()

    def start_quadratic(group, row):
        q_out[group] = jnp.broadcast_to(row, q_out.shape[1:])
        q_copy(group).start()

    def finish_sums(group):
        row = s_out[group, 0:1]
        for index in range(len(group_peers[group])):
            s_copy(group, index).wait_recv()
            row = row + s_in[group, index, 0:1]
        bits = groups[group]
        row = row + rows_found[bits[-1]]
        if len(bits) == 2:
            q_copy(group).wait_recv()
            row = row + (rows_found[bits[0]] + q_in[group, 0:1])
        return row

    rows_found = {}
    for step, bits in enumerate(steps):
        if step == len(steps) - 1 and low > 0:
            base[...] = sums[...] + spread(0, low)
        for tier in range(tiers - 1, bits[0] - 1, -1):
            found = combine(1, step, tier)
            if found is not None:
                rows_found[tier] = row_of(jnp.zeros_like(found), found)
                if tier != groups[tier // 2][-1]:
                    start_quadratic(tier // 2, rows_found[tier])
            if step > 0 and tier == tiers - 1:
                group = steps[step - 1][-1] // 2
                if steps[step - 1][-1] == groups[group][-1]:
                    start_sums(group + 1, finish_sums(group))
            if step == 0 and tier == max(tiers - 2, 0):
                add_partner(1)
                r_now = r_ref[...]
                start_sums(
                    0, row_of(lane_fold(r_now * r_now), lane_fold(r_now * sums[...]))
                )
    dense = base[...] if low > 0 else sums[...]
    image_ref[...] = dense + spread(low, tiers)
    row = finish_sums(len(groups) - 1)
    columns = jnp.broadcast_to(row, (row.shape[1], row.shape[1])).T
    step_ref[...] = columns[:cols] / columns[cols:]

    for turn in range(2):
        z_copy(turn).wait_send()
        w_copy(turn).wait_send()
        for step, bits in enumerate(steps):
            for tier in range(bits[0], tiers):
                for piece in pieces(tier):
                    for index in range(len(step_peers(step, tier))):
                        t_copy(turn, step, tier, piece, index).wait_send()
    for group, peers in enumerate(group_peers):
        for index in range(len(peers)):
            s_copy(group, index).wait_send()
        if len(groups[group]) == 2:
            q_copy(group).wait_send()


def local(rhs_matrix, initial_guess, leaf_blocks, row_bases, couplings):
    tiers, rank, leaf = row_bases.shape
    cols = initial_guess.shape[1]
    half = leaf // 2
    groups = pl.cdiv(tiers, 2)
    padded = pl.cdiv(rank, LANES) * LANES
    assert 2 * cols == LANES and leaf_blocks.shape == (half, leaf)
    assert 2**tiers == lax.axis_size("leaf") and lax.axis_size("rhs") == 2
    any_spec = pl.BlockSpec(memory_space=pl.ANY)
    vmem_spec = pl.BlockSpec(memory_space=pltpu.VMEM)
    vmem, dma = pltpu.VMEM, pltpu.SemaphoreType.DMA
    guess = initial_guess.T
    residual, image, step = pl.pallas_call(
        kernel,
        out_shape=[vmem((cols, leaf), F32), vmem((cols, leaf), F32), vmem((cols, LANES), F32)],
        in_specs=[any_spec] * 5,
        out_specs=[vmem_spec] * 3,
        scratch_shapes=[
            vmem((cols, leaf), F32),
            vmem((cols, leaf), F32),
            vmem((half, leaf), F32),
            vmem((tiers, rank, leaf), F32),
            vmem((tiers, rank, rank), F32),
            vmem((half, leaf), BF16),
            vmem((half, leaf), BF16),
            vmem((tiers, padded, leaf), BF16),
            vmem((tiers, padded, leaf), BF16),
            vmem((tiers, padded, padded), BF16),
            vmem((tiers, padded, padded), BF16),
            vmem((cols, leaf), BF16),
            vmem((cols, leaf), BF16),
            vmem((cols, tiers * padded), BF16),
            vmem((cols, tiers * padded), BF16),
            vmem((cols, leaf), F32),
            vmem((cols, leaf), F32),
            vmem((2, cols, half), F32),
            vmem((2, cols, half), F32),
            vmem((2, cols, half), F32),
            vmem((2, tiers, tiers, cols, padded), F32),
            vmem((2, tiers, tiers, 3, cols, padded), F32),
            vmem((groups, 8, LANES), F32),
            vmem((groups, 3, 8, LANES), F32),
            vmem((groups, 8, LANES), F32),
            vmem((groups, 8, LANES), F32),
            dma((4 + groups,)),
            dma((2,)),
            dma((2,)),
            dma((2,)),
            dma((2,)),
            dma((2, tiers, tiers, 3, PIECES)),
            dma((2, tiers, tiers, 3, PIECES)),
            dma((groups, 3)),
            dma((groups, 3)),
            dma((groups,)),
            dma((groups,)),
        ],
        compiler_params=pltpu.CompilerParams(collective_id=0, has_side_effects=True),
        name="cg_step",
    )(guess, rhs_matrix.T, leaf_blocks, row_bases, couplings)
    alpha = jnp.tile(step, (1, leaf // LANES))
    return (guess + alpha * residual).T, (residual - alpha * image).T


def solution(mesh):
    return jax.shard_map(
        local,
        mesh=mesh,
        in_specs=(
            P("leaf", "rhs"),
            P("leaf", "rhs"),
            P(("leaf", "rhs"), None),
            P(None, None, "leaf"),
            P(),
        ),
        out_specs=(P("leaf", "rhs"), P("leaf", "rhs")),
        check_vma=False,
    )
```

```python
import functools

import jax
import jax.numpy as jnp
from jax import lax
from jax.experimental import pallas as pl
from jax.experimental.pallas import tpu as pltpu
from jax.sharding import PartitionSpec as P

MESH = pl.DeviceIdType.MESH
F32 = jnp.float32
BF16 = jnp.bfloat16
LANES = 128
DIRECT = 8
NN = (((1,), (0,)), ((), ()))
NT = (((1,), (1,)), ((), ()))


def halves(value):
    high = value.astype(BF16)
    return high, (value - high.astype(F32)).astype(BF16)


def dot3(left, right, dims):
    rows = left[0].shape[0]
    stacked = lax.dot_general(
        jnp.concatenate(left, axis=0), right[0], dims, preferred_element_type=F32
    )
    cross = lax.dot_general(left[0], right[1], dims, preferred_element_type=F32)
    return stacked[:rows] + (stacked[rows:] + cross)


def lane_fold(value):
    total = value[:, :LANES]
    for start in range(LANES, value.shape[1], LANES):
        total = total + value[:, start : start + LANES]
    return total


def masks_over(low, high):
    return [value << low for value in range(2 ** (high - low) - 1, 0, -1)]


def plan_of(tier):
    if 2 ** (tier + 1) <= DIRECT:
        return [masks_over(0, tier + 1)]
    return [masks_over(low, min(low + 2, tier + 1)) for low in range(0, tier + 1, 2)]


def flip(leaf_index, mask):
    bit = 1
    while bit <= mask:
        if mask & bit:
            leaf_index = leaf_index + bit * (1 - 2 * ((leaf_index // bit) % 2))
        bit *= 2
    return leaf_index


def pack_shape(cols, rank):
    padded = pl.cdiv(rank, LANES) * LANES
    spare = padded - rank
    if padded != LANES or not spare or rank % spare or cols * spare % (8 * LANES):
        return cols, padded
    return cols * rank // LANES, LANES


def pack(value, rank):
    cols, padded = value.shape
    keep = pack_shape(cols, rank)[0]
    if keep == cols:
        return value
    spare = padded - rank
    extra = value[keep:]
    moved = [
        pltpu.roll(extra, (rank - start) % padded, axis=1) for start in range(0, rank, spare)
    ]
    lane = lax.broadcasted_iota(jnp.int32, (keep, padded), 1)
    return jnp.where(lane < rank, value[:keep], jnp.concatenate(moved, axis=0))


def unpack(value, cols, rank):
    keep, padded = value.shape
    if keep == cols:
        return value
    spare = padded - rank
    count = cols - keep
    lane = lax.broadcasted_iota(jnp.int32, (count, padded), 1)
    extra = jnp.zeros((count, padded), F32)
    for index, start in enumerate(range(0, rank, spare)):
        part = pltpu.roll(
            value[index * count : (index + 1) * count], (start - rank) % padded, axis=1
        )
        extra = jnp.where((lane >= start) & (lane < start + spare), part, extra)
    lane = lax.broadcasted_iota(jnp.int32, (keep, padded), 1)
    return jnp.concatenate([jnp.where(lane < rank, value, 0.0), extra], axis=0)


def row_of(upper, lower):
    stacked = jnp.concatenate([upper, lower], axis=0)
    return jnp.sum(stacked.T, axis=0, keepdims=True)


def kernel(
    x_hbm, b_hbm, d_hbm, u_hbm, c_hbm,
    r_ref, image_ref, step_ref,
    x_v, b_v, d_v, e_v, u_v, c_v,
    d_hi, d_lo, e_hi, e_lo, u_hi, u_lo, c_hi, c_lo, w_hi, w_lo, v_hi, v_lo, cc_hi, cc_lo,
    sums, base, t_out, t_in, s_out, s_in, q_out, q_in,
    local_sem, e_send, e_recv, t_send, t_recv, s_send, s_recv, q_send, q_recv,
):
    tiers, rank, leaf = u_v.shape
    cols = x_v.shape[0]
    half = leaf // 2
    padded = u_hi.shape[1]
    me, core = lax.axis_index("leaf"), lax.axis_index("rhs")
    other = 1 - core
    mine = pl.ds(pl.multiple_of(core * half, half), half)
    theirs = pl.ds(pl.multiple_of(other * half, half), half)
    plans = [plan_of(tier) for tier in range(tiers)]
    low = sum(len(plan) == 1 for plan in plans)
    everyone = masks_over(0, tiers)

    barrier = pltpu.get_barrier_semaphore()
    for target in [(flip(me, mask), core) for mask in everyone] + [(me, other)]:
        pl.semaphore_signal(barrier, inc=1, device_id=target, device_id_type=MESH)

    arrays = [(x_hbm, x_v)]
    arrays += [(u_hbm.at[tier], u_v.at[tier]) for tier in reversed(range(tiers))]
    arrays += [(d_hbm, d_v), (c_hbm, c_v), (b_hbm, b_v)]
    loads = [
        pltpu.make_async_copy(source, target, local_sem.at[index])
        for index, (source, target) in enumerate(arrays)
    ]
    for load in loads:
        load.start()
    x_load, *u_loads, d_load, c_load, b_load = loads

    def remote(source, target, send, recv, device):
        return pltpu.make_async_remote_copy(
            src_ref=source, dst_ref=target, send_sem=send, recv_sem=recv,
            device_id=device, device_id_type=MESH,
        )

    e_copy = remote(d_hbm.at[:, mine], e_v, e_send, e_recv, (me, other))

    def t_copies(turn, tier, stage):
        at = (turn, tier, stage)
        return [
            remote(
                t_out.at[at], t_in.at[(*at, index)], t_send.at[at], t_recv.at[at],
                (flip(me, mask), core),
            )
            for index, mask in enumerate(plans[tier][stage])
        ]

    def s_copies():
        return [
            remote(s_out, s_in.at[index], s_send, s_recv, (flip(me, mask), core))
            for index, mask in enumerate(everyone)
        ]

    def q_copies(tier):
        return [
            remote(
                q_out.at[tier], q_in.at[tier, index], q_send.at[tier], q_recv.at[tier],
                (flip(me, mask), core),
            )
            for index, mask in enumerate(masks_over(tier + 1, tiers))
        ]

    def start(copies):
        for copy in copies:
            copy.start()

    def wait_all(buffer, sem):
        pltpu.make_async_copy(buffer, buffer, sem).wait()

    if padded > rank:
        blank = jnp.zeros((tiers, padded - rank, leaf), BF16)
        u_hi[:, rank:, :] = blank
        u_lo[:, rank:, :] = blank
    c_hi[...] = jnp.zeros_like(c_hi)
    c_lo[...] = jnp.zeros_like(c_lo)

    def project(turn, tier):
        products = dot3((v_hi[...], v_lo[...]), (u_hi[tier], u_lo[tier]), NT)
        t_out[turn, tier, 0] = pack(products, rank)

    def gathered(turn, tier, stage):
        count = len(plans[tier][stage])
        into = t_in.at[turn, tier, stage, :count]
        wait_all(into, t_recv.at[turn, tier, stage])
        return t_out[turn, tier, stage] + jnp.sum(into[...], axis=0)

    def forward(turn, tier, stage):
        t_out[turn, tier, stage + 1] = gathered(turn, tier, stage)
        start(t_copies(turn, tier, stage + 1))

    def total_of(turn, tier):
        return unpack(gathered(turn, tier, len(plans[tier]) - 1), cols, rank)

    def couple(tier, total):
        return dot3(total, (c_hi[tier], c_lo[tier]), NT)

    def place(tier, value):
        at = slice(tier * padded, (tier + 1) * padded)
        cc_hi[:, at], cc_lo[:, at] = value

    def spread(first, last, parts):
        at = slice(first * padded, last * padded)
        count = (last - first) * padded
        return dot3(
            (cc_hi[:, at], cc_lo[:, at]),
            tuple(part.reshape(count, leaf) for part in parts),
            NN,
        )

    def spread_low():
        return spread(0, low, (u_hi[:low], u_lo[:low]))

    def spread_high():
        return spread(low, tiers, (w_hi[...], w_lo[...]))

    def dense_own():
        sums[:, mine] = dot3((v_hi[...], v_lo[...]), (d_hi[...], d_lo[...]), NT)
        sums[:, theirs] = dot3(
            (v_hi[:, mine], v_lo[:, mine]), (d_hi[:, theirs], d_lo[:, theirs]), NN
        )

    def dense_rest():
        sums[:, theirs] = sums[:, theirs] + dot3(
            (v_hi[:, theirs], v_lo[:, theirs]), (e_hi[...], e_lo[...]), NN
        )

    stages = len(plans[-1])

    x_load.wait()
    v_hi[...], v_lo[...] = halves(x_v[...])
    for index, tier in enumerate(reversed(range(tiers))):
        u_loads[index].wait()
        u_hi[tier, :rank], u_lo[tier, :rank] = halves(u_v[tier])
        project(0, tier)
        if index == 0:
            pl.semaphore_wait(barrier, len(everyone) + 1)
        start(t_copies(0, tier, 0))
        if index == 0:
            e_copy.start()
    d_load.wait()
    d_hi[...], d_lo[...] = halves(d_v[...])
    dense_own()
    c_load.wait()
    c_hi[:, :rank, :rank], c_lo[:, :rank, :rank] = halves(c_v[...])
    for tier in range(low, tiers):
        w_hi[tier - low], w_lo[tier - low] = halves(
            dot3((c_hi[tier], c_lo[tier]), (u_hi[tier], u_lo[tier]), NN)
        )
    for stage in range(stages - 1):
        for tier in reversed(range(low, tiers)):
            if stage + 1 < len(plans[tier]):
                forward(0, tier, stage)
        if stage == 0:
            e_copy.wait_recv()
            e_hi[...], e_lo[...] = halves(e_v[...])
            dense_rest()
            b_load.wait()
            base[...] = b_v[...] - sums[...]
            for tier in range(low):
                place(tier, halves(couple(tier, halves(total_of(0, tier)))))
            base[...] = base[...] - spread_low()
    for tier in range(low, tiers):
        place(tier, halves(total_of(0, tier)))
    residual = base[...] - spread_high()
    r_ref[...] = residual
    v_hi[...], v_lo[...] = halves(residual)

    for tier in reversed(range(tiers)):
        project(1, tier)
        start(t_copies(1, tier, 0))
    dense_own()
    dense_rest()
    r_now = r_ref[...]
    rows = [row_of(lane_fold(r_now * r_now), lane_fold(r_now * sums[...]))]
    s_out[...] = jnp.broadcast_to(rows[0], s_out.shape)
    start(s_copies())

    def quadratic(tier, total):
        coupled = couple(tier, halves(total))
        found = lane_fold(total * coupled)
        rows.append(row_of(jnp.zeros_like(found), found))
        if tier < tiers - 1:
            q_out[tier] = jnp.broadcast_to(rows[-1], q_out.shape[1:])
            start(q_copies(tier))
        return coupled

    for stage in range(stages - 1):
        for tier in reversed(range(low, tiers)):
            if stage + 1 < len(plans[tier]):
                forward(1, tier, stage)
        if stage == 0:
            for tier in range(low):
                place(tier, halves(quadratic(tier, total_of(1, tier))))
            base[...] = sums[...] + spread_low()
    for tier in range(low, tiers):
        total = total_of(1, tier)
        place(tier, halves(total))
        quadratic(tier, total)
    image_ref[...] = base[...] + spread_high()
    wait_all(s_in, s_recv)
    row = jnp.sum(s_in[...], axis=0)
    for tier in range(tiers - 1):
        into = q_in.at[tier, : len(masks_over(tier + 1, tiers))]
        wait_all(into, q_recv.at[tier])
        row = row + jnp.sum(into[...], axis=0)
    row = row[:1] + sum(rows)
    columns = jnp.broadcast_to(row, (row.shape[1], row.shape[1])).T
    step_ref[...] = columns[:cols] / columns[cols:]

    e_copy.wait_send()
    for turn in range(2):
        for tier, plan in enumerate(plans):
            for stage in range(len(plan)):
                for copy in t_copies(turn, tier, stage):
                    copy.wait_send()
    for copy in s_copies():
        copy.wait_send()
    for tier in range(tiers - 1):
        for copy in q_copies(tier):
            copy.wait_send()


def local(rhs_matrix, initial_guess, leaf_blocks, row_bases, couplings):
    tiers, rank, leaf = row_bases.shape
    cols = initial_guess.shape[1]
    half = leaf // 2
    padded = pl.cdiv(rank, LANES) * LANES
    plans = [plan_of(tier) for tier in range(tiers)]
    low = sum(len(plan) == 1 for plan in plans)
    stages, most = len(plans[-1]), max(len(masks) for plan in plans for masks in plan)
    assert 2 * cols == LANES and leaf_blocks.shape == (half, leaf) and low < tiers
    assert 2**tiers == lax.axis_size("leaf") and lax.axis_size("rhs") == 2
    any_spec = pl.BlockSpec(memory_space=pl.ANY)
    vmem_spec = pl.BlockSpec(memory_space=pltpu.VMEM)
    vmem, dma = pltpu.VMEM, pltpu.SemaphoreType.DMA
    packed = pack_shape(cols, rank)
    guess = initial_guess.T
    residual, image, step = pl.pallas_call(
        kernel,
        out_shape=[vmem((cols, leaf), F32), vmem((cols, leaf), F32), vmem((cols, LANES), F32)],
        in_specs=[any_spec] * 5,
        out_specs=[vmem_spec] * 3,
        scratch_shapes=[
            vmem((cols, leaf), F32),
            vmem((cols, leaf), F32),
            vmem((half, leaf), F32),
            vmem((half, half), F32),
            vmem((tiers, rank, leaf), F32),
            vmem((tiers, rank, rank), F32),
            vmem((half, leaf), BF16),
            vmem((half, leaf), BF16),
            vmem((half, half), BF16),
            vmem((half, half), BF16),
            vmem((tiers, padded, leaf), BF16),
            vmem((tiers, padded, leaf), BF16),
            vmem((tiers, padded, padded), BF16),
            vmem((tiers, padded, padded), BF16),
            vmem((tiers - low, padded, leaf), BF16),
            vmem((tiers - low, padded, leaf), BF16),
            vmem((cols, leaf), BF16),
            vmem((cols, leaf), BF16),
            vmem((cols, tiers * padded), BF16),
            vmem((cols, tiers * padded), BF16),
            vmem((cols, leaf), F32),
            vmem((cols, leaf), F32),
            vmem((2, tiers, stages, *packed), F32),
            vmem((2, tiers, stages, most, *packed), F32),
            vmem((8, LANES), F32),
            vmem((2**tiers - 1, 8, LANES), F32),
            vmem((tiers, 8, LANES), F32),
            vmem((tiers, 2 ** (tiers - 1) - 1, 8, LANES), F32),
            dma((4 + tiers,)),
            dma,
            dma,
            dma((2, tiers, stages)),
            dma((2, tiers, stages)),
            dma,
            dma,
            dma((tiers,)),
            dma((tiers,)),
        ],
        compiler_params=pltpu.CompilerParams(collective_id=0, has_side_effects=True),
        name="cg_step",
    )(guess, rhs_matrix.T, leaf_blocks, row_bases, couplings)
    alpha = jnp.tile(step, (1, leaf // LANES))
    return (guess + alpha * residual).T, (residual - alpha * image).T


def solution(mesh):
    return jax.shard_map(
        local,
        mesh=mesh,
        in_specs=(
            P("leaf", "rhs"),
            P("leaf", "rhs"),
            P(("leaf", "rhs"), None),
            P(None, None, "leaf"),
            P(),
        ),
        out_specs=(P("leaf", "rhs"), P("leaf", "rhs")),
        check_vma=False,
    )
```

```python
import functools

import jax
import jax.numpy as jnp
from jax import lax
from jax.experimental import pallas as pl
from jax.experimental.pallas import tpu as pltpu
from jax.sharding import PartitionSpec as P

MESH = pl.DeviceIdType.MESH
F32 = jnp.float32
BF16 = jnp.bfloat16
LANES = 128
DIRECT = 8
NN = (((1,), (0,)), ((), ()))
NT = (((1,), (1,)), ((), ()))


def halves(value):
    high = value.astype(BF16)
    return high, (value - high.astype(F32)).astype(BF16)


def dot3(left, right, dims):
    rows = left[0].shape[0]
    stacked = lax.dot_general(
        jnp.concatenate(left, axis=0), right[0], dims, preferred_element_type=F32
    )
    cross = lax.dot_general(left[0], right[1], dims, preferred_element_type=F32)
    return stacked[:rows] + (stacked[rows:] + cross)


def lane_fold(value):
    total = value[:, :LANES]
    for start in range(LANES, value.shape[1], LANES):
        total = total + value[:, start : start + LANES]
    return total


def masks_over(low, high):
    return [value << low for value in range(2 ** (high - low) - 1, 0, -1)]


def plan_of(tier):
    if 2 ** (tier + 1) <= DIRECT:
        return [masks_over(0, tier + 1)]
    return [masks_over(low, min(low + 2, tier + 1)) for low in range(0, tier + 1, 2)]


def flip(leaf_index, mask):
    bit = 1
    while bit <= mask:
        if mask & bit:
            leaf_index = leaf_index + bit * (1 - 2 * ((leaf_index // bit) % 2))
        bit *= 2
    return leaf_index


def pack_shape(cols, rank):
    padded = pl.cdiv(rank, LANES) * LANES
    spare = padded - rank
    if padded != LANES or not spare or rank % spare or cols * spare % (8 * LANES):
        return cols, padded
    return cols * rank // LANES, LANES


def pack(value, rank):
    cols, padded = value.shape
    keep = pack_shape(cols, rank)[0]
    if keep == cols:
        return value
    spare = padded - rank
    extra = value[keep:]
    moved = [
        pltpu.roll(extra, (rank - start) % padded, axis=1) for start in range(0, rank, spare)
    ]
    lane = lax.broadcasted_iota(jnp.int32, (keep, padded), 1)
    return jnp.where(lane < rank, value[:keep], jnp.concatenate(moved, axis=0))


def unpack(value, cols, rank):
    keep, padded = value.shape
    if keep == cols:
        return value
    spare = padded - rank
    count = cols - keep
    lane = lax.broadcasted_iota(jnp.int32, (count, padded), 1)
    extra = jnp.zeros((count, padded), F32)
    for index, start in enumerate(range(0, rank, spare)):
        part = pltpu.roll(
            value[index * count : (index + 1) * count], (start - rank) % padded, axis=1
        )
        extra = jnp.where((lane >= start) & (lane < start + spare), part, extra)
    lane = lax.broadcasted_iota(jnp.int32, (keep, padded), 1)
    return jnp.concatenate([jnp.where(lane < rank, value, 0.0), extra], axis=0)


def row_of(upper, lower):
    stacked = jnp.concatenate([upper, lower], axis=0)
    return jnp.sum(stacked.T, axis=0, keepdims=True)


def kernel(
    x_hbm, b_hbm, d_hbm, u_hbm, c_hbm,
    r_ref, image_ref, step_ref,
    x_v, b_v, d_v, e_v, u_v, c_v,
    d_hi, d_lo, e_hi, e_lo, u_hi, u_lo, c_hi, c_lo, w_hi, w_lo, v_hi, v_lo, cc_hi, cc_lo,
    sums, base, t_out, t_in, s_out, s_in, q_out, q_in,
    local_sem, e_send, e_recv, t_send, t_recv, s_send, s_recv, q_send, q_recv,
):
    tiers, rank, leaf = u_v.shape
    cols = x_v.shape[0]
    half = leaf // 2
    padded = u_hi.shape[1]
    me, core = lax.axis_index("leaf"), lax.axis_index("rhs")
    other = 1 - core
    mine = pl.ds(pl.multiple_of(core * half, half), half)
    theirs = pl.ds(pl.multiple_of(other * half, half), half)
    plans = [plan_of(tier) for tier in range(tiers)]
    low = sum(len(plan) == 1 for plan in plans)
    everyone = masks_over(0, tiers)

    barrier = pltpu.get_barrier_semaphore()
    for target in [(flip(me, mask), core) for mask in everyone] + [(me, other)]:
        pl.semaphore_signal(barrier, inc=1, device_id=target, device_id_type=MESH)

    arrays = [(x_hbm, x_v)]
    arrays += [(u_hbm.at[tier], u_v.at[tier]) for tier in reversed(range(tiers))]
    arrays += [(d_hbm, d_v), (c_hbm, c_v), (b_hbm, b_v)]
    loads = [
        pltpu.make_async_copy(source, target, local_sem.at[index])
        for index, (source, target) in enumerate(arrays)
    ]
    for load in loads:
        load.start()
    x_load, *u_loads, d_load, c_load, b_load = loads

    def remote(source, target, send, recv, device):
        return pltpu.make_async_remote_copy(
            src_ref=source, dst_ref=target, send_sem=send, recv_sem=recv,
            device_id=device, device_id_type=MESH,
        )

    e_copy = remote(d_hbm.at[:, mine], e_v, e_send, e_recv, (me, other))

    def t_copies(turn, tier, stage):
        at = (turn, tier, stage)
        return [
            remote(
                t_out.at[at], t_in.at[(*at, index)], t_send.at[at], t_recv.at[at],
                (flip(me, mask), core),
            )
            for index, mask in enumerate(plans[tier][stage])
        ]

    def s_copies():
        return [
            remote(s_out, s_in.at[index], s_send, s_recv, (flip(me, mask), core))
            for index, mask in enumerate(everyone)
        ]

    def q_copies(tier):
        return [
            remote(
                q_out.at[tier], q_in.at[tier, index], q_send.at[tier], q_recv.at[tier],
                (flip(me, mask), core),
            )
            for index, mask in enumerate(masks_over(tier + 1, tiers))
        ]

    def start(copies):
        for copy in copies:
            copy.start()

    def wait_all(buffer, sem):
        pltpu.make_async_copy(buffer, buffer, sem).wait()

    if padded > rank:
        blank = jnp.zeros((tiers, padded - rank, leaf), BF16)
        u_hi[:, rank:, :] = blank
        u_lo[:, rank:, :] = blank
    c_hi[...] = jnp.zeros_like(c_hi)
    c_lo[...] = jnp.zeros_like(c_lo)

    def project(turn, tier):
        products = dot3((v_hi[...], v_lo[...]), (u_hi[tier], u_lo[tier]), NT)
        t_out[turn, tier, 0] = pack(products, rank)

    def gathered(turn, tier, stage):
        count = len(plans[tier][stage])
        into = t_in.at[turn, tier, stage, :count]
        wait_all(into, t_recv.at[turn, tier, stage])
        return t_out[turn, tier, stage] + jnp.sum(into[...], axis=0)

    def forward(turn, tier, stage):
        t_out[turn, tier, stage + 1] = gathered(turn, tier, stage)
        start(t_copies(turn, tier, stage + 1))

    def total_of(turn, tier):
        return unpack(gathered(turn, tier, len(plans[tier]) - 1), cols, rank)

    def couple(tier, total):
        return dot3(total, (c_hi[tier], c_lo[tier]), NT)

    def place(tier, value):
        at = slice(tier * padded, (tier + 1) * padded)
        cc_hi[:, at], cc_lo[:, at] = value

    def spread(first, last, parts):
        at = slice(first * padded, last * padded)
        count = (last - first) * padded
        return dot3(
            (cc_hi[:, at], cc_lo[:, at]),
            tuple(part.reshape(count, leaf) for part in parts),
            NN,
        )

    def spread_low():
        return spread(0, low, (u_hi[:low], u_lo[:low]))

    def spread_high():
        return spread(low, tiers, (w_hi[...], w_lo[...]))

    def dense_own():
        sums[:, mine] = dot3((v_hi[...], v_lo[...]), (d_hi[...], d_lo[...]), NT)
        sums[:, theirs] = dot3(
            (v_hi[:, mine], v_lo[:, mine]), (d_hi[:, theirs], d_lo[:, theirs]), NN
        )

    def dense_rest():
        sums[:, theirs] = sums[:, theirs] + dot3(
            (v_hi[:, theirs], v_lo[:, theirs]), (e_hi[...], e_lo[...]), NN
        )

    stages = len(plans[-1])

    x_load.wait()
    v_hi[...], v_lo[...] = halves(x_v[...])
    for index, tier in enumerate(reversed(range(tiers))):
        u_loads[tiers - 1 - tier].wait()
        u_hi[tier, :rank], u_lo[tier, :rank] = halves(u_v[tier])
        project(0, tier)
        if index == 0:
            pl.semaphore_wait(barrier, len(everyone) + 1)
        start(t_copies(0, tier, 0))
        if index == 0:
            e_copy.start()
    d_load.wait()
    d_hi[...], d_lo[...] = halves(d_v[...])
    dense_own()
    c_load.wait()
    c_hi[:, :rank, :rank], c_lo[:, :rank, :rank] = halves(c_v[...])
    for tier in range(low, tiers):
        w_hi[tier - low], w_lo[tier - low] = halves(
            dot3((c_hi[tier], c_lo[tier]), (u_hi[tier], u_lo[tier]), NN)
        )
    for stage in range(stages - 1):
        for tier in reversed(range(low, tiers)):
            if stage + 1 < len(plans[tier]):
                forward(0, tier, stage)
        if stage == 0:
            e_copy.wait_recv()
            e_hi[...], e_lo[...] = halves(e_v[...])
            dense_rest()
            b_load.wait()
            base[...] = b_v[...] - sums[...]
            for tier in range(low):
                place(tier, halves(couple(tier, halves(total_of(0, tier)))))
            base[...] = base[...] - spread_low()
    for tier in range(low, tiers):
        place(tier, halves(total_of(0, tier)))
    residual = base[...] - spread_high()
    r_ref[...] = residual
    v_hi[...], v_lo[...] = halves(residual)

    for tier in reversed(range(low, tiers)):
        project(1, tier)
        start(t_copies(1, tier, 0))
    blocks = tuple(part[:low].reshape(low * padded, leaf) for part in (u_hi, u_lo))
    products = dot3((v_hi[...], v_lo[...]), blocks, NT)
    for tier in range(low):
        t_out[1, tier, 0] = pack(products[:, tier * padded : (tier + 1) * padded], rank)
        start(t_copies(1, tier, 0))
    dense_own()
    dense_rest()
    r_now = r_ref[...]
    rows = [row_of(lane_fold(r_now * r_now), lane_fold(r_now * sums[...]))]
    s_out[...] = rows[0]
    start(s_copies())

    def quadratic(tier, total):
        coupled = couple(tier, halves(total))
        found = lane_fold(total * coupled)
        rows.append(row_of(jnp.zeros_like(found), found))
        if tier < tiers - 1:
            q_out[tier] = rows[-1]
            start(q_copies(tier))
        return coupled

    for stage in range(stages - 1):
        for tier in reversed(range(low, tiers)):
            if stage + 1 < len(plans[tier]):
                forward(1, tier, stage)
        if stage == 0:
            for tier in range(low):
                place(tier, halves(quadratic(tier, total_of(1, tier))))
            base[...] = sums[...] + spread_low()
    for tier in range(low, tiers):
        total = total_of(1, tier)
        place(tier, halves(total))
        quadratic(tier, total)
    image_ref[...] = base[...] + spread_high()
    wait_all(s_in, s_recv)
    row = jnp.sum(s_in[...], axis=0)
    for tier in range(tiers - 1):
        into = q_in.at[tier, : len(masks_over(tier + 1, tiers))]
        wait_all(into, q_recv.at[tier])
        row = row + jnp.sum(into[...], axis=0)
    row = row + sum(rows)
    columns = jnp.broadcast_to(row, (row.shape[1], row.shape[1])).T
    step_ref[...] = columns[:cols] / columns[cols:]

    e_copy.wait_send()
    for turn in range(2):
        for tier, plan in enumerate(plans):
            for stage in range(len(plan)):
                for copy in t_copies(turn, tier, stage):
                    copy.wait_send()
    for copy in s_copies():
        copy.wait_send()
    for tier in range(tiers - 1):
        for copy in q_copies(tier):
            copy.wait_send()


def local(rhs_matrix, initial_guess, leaf_blocks, row_bases, couplings):
    tiers, rank, leaf = row_bases.shape
    cols = initial_guess.shape[1]
    half = leaf // 2
    padded = pl.cdiv(rank, LANES) * LANES
    plans = [plan_of(tier) for tier in range(tiers)]
    low = sum(len(plan) == 1 for plan in plans)
    stages, most = len(plans[-1]), max(len(masks) for plan in plans for masks in plan)
    assert 2 * cols == LANES and leaf_blocks.shape == (half, leaf) and low < tiers
    assert 2**tiers == lax.axis_size("leaf") and lax.axis_size("rhs") == 2
    any_spec = pl.BlockSpec(memory_space=pl.ANY)
    vmem_spec = pl.BlockSpec(memory_space=pltpu.VMEM)
    vmem, dma = pltpu.VMEM, pltpu.SemaphoreType.DMA
    packed = pack_shape(cols, rank)
    guess = initial_guess.T
    residual, image, step = pl.pallas_call(
        kernel,
        out_shape=[vmem((cols, leaf), F32), vmem((cols, leaf), F32), vmem((cols, LANES), F32)],
        in_specs=[any_spec] * 5,
        out_specs=[vmem_spec] * 3,
        scratch_shapes=[
            vmem((cols, leaf), F32),
            vmem((cols, leaf), F32),
            vmem((half, leaf), F32),
            vmem((half, half), F32),
            vmem((tiers, rank, leaf), F32),
            vmem((tiers, rank, rank), F32),
            vmem((half, leaf), BF16),
            vmem((half, leaf), BF16),
            vmem((half, half), BF16),
            vmem((half, half), BF16),
            vmem((tiers, padded, leaf), BF16),
            vmem((tiers, padded, leaf), BF16),
            vmem((tiers, padded, padded), BF16),
            vmem((tiers, padded, padded), BF16),
            vmem((tiers - low, padded, leaf), BF16),
            vmem((tiers - low, padded, leaf), BF16),
            vmem((cols, leaf), BF16),
            vmem((cols, leaf), BF16),
            vmem((cols, tiers * padded), BF16),
            vmem((cols, tiers * padded), BF16),
            vmem((cols, leaf), F32),
            vmem((cols, leaf), F32),
            vmem((2, tiers, stages, *packed), F32),
            vmem((2, tiers, stages, most, *packed), F32),
            vmem((1, LANES), F32),
            vmem((2**tiers - 1, 1, LANES), F32),
            vmem((tiers, 1, LANES), F32),
            vmem((tiers, 2 ** (tiers - 1) - 1, 1, LANES), F32),
            dma((4 + tiers,)),
            dma,
            dma,
            dma((2, tiers, stages)),
            dma((2, tiers, stages)),
            dma,
            dma,
            dma((tiers,)),
            dma((tiers,)),
        ],
        compiler_params=pltpu.CompilerParams(collective_id=0, has_side_effects=True),
        name="cg_step",
    )(guess, rhs_matrix.T, leaf_blocks, row_bases, couplings)
    alpha = jnp.tile(step, (1, leaf // LANES))
    return (guess + alpha * residual).T, (residual - alpha * image).T


def solution(mesh):
    return jax.shard_map(
        local,
        mesh=mesh,
        in_specs=(
            P("leaf", "rhs"),
            P("leaf", "rhs"),
            P(("leaf", "rhs"), None),
            P(None, None, "leaf"),
            P(),
        ),
        out_specs=(P("leaf", "rhs"), P("leaf", "rhs")),
        check_vma=False,
    )
```

```python
import functools

import jax
import jax.numpy as jnp
from jax import lax
from jax.experimental import pallas as pl
from jax.experimental.pallas import tpu as pltpu
from jax.sharding import PartitionSpec as P

MESH = pl.DeviceIdType.MESH
F32 = jnp.float32
BF16 = jnp.bfloat16
LANES = 128
DIRECT = 8
NN = (((1,), (0,)), ((), ()))
NT = (((1,), (1,)), ((), ()))


def halves(value):
    high = value.astype(BF16)
    return high, (value - high.astype(F32)).astype(BF16)


def dot3(left, right, dims):
    rows = left[0].shape[0]
    stacked = lax.dot_general(
        jnp.concatenate(left, axis=0), right[0], dims, preferred_element_type=F32
    )
    cross = lax.dot_general(left[0], right[1], dims, preferred_element_type=F32)
    return stacked[:rows] + (stacked[rows:] + cross)


def lane_fold(value):
    total = value[:, :LANES]
    for start in range(LANES, value.shape[1], LANES):
        total = total + value[:, start : start + LANES]
    return total


def masks_over(low, high):
    return [value << low for value in range(2 ** (high - low) - 1, 0, -1)]


def plan_of(turn, tier):
    if turn == 1 and 2 ** (tier + 1) <= DIRECT:
        return [masks_over(0, tier + 1)]
    return [masks_over(low, min(low + 2, tier + 1)) for low in range(0, tier + 1, 2)]


def flip(leaf_index, mask):
    bit = 1
    while bit <= mask:
        if mask & bit:
            leaf_index = leaf_index + bit * (1 - 2 * ((leaf_index // bit) % 2))
        bit *= 2
    return leaf_index


def pack_shape(cols, rank):
    padded = pl.cdiv(rank, LANES) * LANES
    spare = padded - rank
    if padded != LANES or not spare or rank % spare or cols * spare % (8 * LANES):
        return cols, padded
    return cols * rank // LANES, LANES


def pack(value, rank):
    cols, padded = value.shape
    keep = pack_shape(cols, rank)[0]
    if keep == cols:
        return value
    spare = padded - rank
    extra = value[keep:]
    moved = [
        pltpu.roll(extra, (rank - start) % padded, axis=1) for start in range(0, rank, spare)
    ]
    lane = lax.broadcasted_iota(jnp.int32, (keep, padded), 1)
    return jnp.where(lane < rank, value[:keep], jnp.concatenate(moved, axis=0))


def unpack(value, cols, rank):
    keep, padded = value.shape
    if keep == cols:
        return value
    spare = padded - rank
    count = cols - keep
    lane = lax.broadcasted_iota(jnp.int32, (count, padded), 1)
    extra = jnp.zeros((count, padded), F32)
    for index, start in enumerate(range(0, rank, spare)):
        part = pltpu.roll(
            value[index * count : (index + 1) * count], (start - rank) % padded, axis=1
        )
        extra = jnp.where((lane >= start) & (lane < start + spare), part, extra)
    lane = lax.broadcasted_iota(jnp.int32, (keep, padded), 1)
    return jnp.concatenate([jnp.where(lane < rank, value, 0.0), extra], axis=0)


def row_of(upper, lower):
    stacked = jnp.concatenate([upper, lower], axis=0)
    return jnp.sum(stacked.T, axis=0, keepdims=True)


def kernel(
    x_hbm, b_hbm, d_hbm, u_hbm, c_hbm,
    r_ref, image_ref, step_ref,
    x_v, b_v, d_v, e_v, u_v, c_v,
    d_hi, d_lo, e_hi, e_lo, u_hi, u_lo, c_hi, c_lo, w_hi, w_lo, v_hi, v_lo, cc_hi, cc_lo,
    sums, base, t_out, t_in, s_out, s_in, q_out, q_in,
    local_sem, e_send, e_recv, t_send, t_recv, s_send, s_recv, q_send, q_recv,
):
    tiers, rank, leaf = u_v.shape
    cols = x_v.shape[0]
    half = leaf // 2
    padded = u_hi.shape[1]
    me, core = lax.axis_index("leaf"), lax.axis_index("rhs")
    other = 1 - core
    mine = pl.ds(pl.multiple_of(core * half, half), half)
    theirs = pl.ds(pl.multiple_of(other * half, half), half)
    plans = [[plan_of(turn, tier) for tier in range(tiers)] for turn in range(2)]
    first, low = [sum(len(plan) == 1 for plan in each) for each in plans]
    everyone = masks_over(0, tiers)
    near = [mask for masks in plans[0][-1] for mask in reversed(masks)]

    barrier = pltpu.get_barrier_semaphore()
    for target in [(flip(me, mask), core) for mask in near] + [(me, other)]:
        pl.semaphore_signal(barrier, inc=1, device_id=target, device_id_type=MESH)

    arrays = [(x_hbm, x_v)]
    arrays += [(u_hbm.at[tier], u_v.at[tier]) for tier in reversed(range(tiers))]
    arrays += [(d_hbm, d_v), (c_hbm, c_v), (b_hbm, b_v)]
    loads = [
        pltpu.make_async_copy(source, target, local_sem.at[index])
        for index, (source, target) in enumerate(arrays)
    ]
    for load in loads:
        load.start()
    x_load, *u_loads, d_load, c_load, b_load = loads

    def remote(source, target, send, recv, device):
        return pltpu.make_async_remote_copy(
            src_ref=source, dst_ref=target, send_sem=send, recv_sem=recv,
            device_id=device, device_id_type=MESH,
        )

    e_copy = remote(d_hbm.at[:, mine], e_v, e_send, e_recv, (me, other))

    def t_copies(turn, tier, stage):
        at = (turn, tier, stage)
        return [
            remote(
                t_out.at[at], t_in.at[(*at, index)], t_send.at[at], t_recv.at[at],
                (flip(me, mask), core),
            )
            for index, mask in enumerate(plans[turn][tier][stage])
        ]

    def s_copies():
        return [
            remote(s_out, s_in.at[index], s_send, s_recv, (flip(me, mask), core))
            for index, mask in enumerate(everyone)
        ]

    def q_copies(tier):
        return [
            remote(
                q_out.at[tier], q_in.at[tier, index], q_send.at[tier], q_recv.at[tier],
                (flip(me, mask), core),
            )
            for index, mask in enumerate(masks_over(tier + 1, tiers))
        ]

    def start(copies):
        for copy in copies:
            copy.start()

    def wait_all(buffer, sem):
        pltpu.make_async_copy(buffer, buffer, sem).wait()

    if padded > rank:
        blank = jnp.zeros((tiers, padded - rank, leaf), BF16)
        u_hi[:, rank:, :] = blank
        u_lo[:, rank:, :] = blank
    c_hi[...] = jnp.zeros_like(c_hi)
    c_lo[...] = jnp.zeros_like(c_lo)

    def project(turn, tier):
        products = dot3((v_hi[...], v_lo[...]), (u_hi[tier], u_lo[tier]), NT)
        t_out[turn, tier, 0] = pack(products, rank)

    def gathered(turn, tier, stage):
        count = len(plans[turn][tier][stage])
        into = t_in.at[turn, tier, stage, :count]
        wait_all(into, t_recv.at[turn, tier, stage])
        return t_out[turn, tier, stage] + jnp.sum(into[...], axis=0)

    def sent(turn, tier, stage):
        count = len(plans[turn][tier][stage])
        wait_all(t_in.at[turn, tier, stage, :count], t_send.at[turn, tier, stage])

    def forward(turn, tier, stage):
        t_out[turn, tier, stage + 1] = gathered(turn, tier, stage)
        start(t_copies(turn, tier, stage + 1))

    def total_of(turn, tier):
        return unpack(gathered(turn, tier, len(plans[turn][tier]) - 1), cols, rank)

    def couple(tier, total):
        return dot3(total, (c_hi[tier], c_lo[tier]), NT)

    def place(tier, value):
        at = slice(tier * padded, (tier + 1) * padded)
        cc_hi[:, at], cc_lo[:, at] = value

    def spread(first, last, parts):
        at = slice(first * padded, last * padded)
        count = (last - first) * padded
        return dot3(
            (cc_hi[:, at], cc_lo[:, at]),
            tuple(part.reshape(count, leaf) for part in parts),
            NN,
        )

    def spread_low():
        return spread(0, low, (u_hi[:low], u_lo[:low]))

    def spread_high():
        return spread(low, tiers, (w_hi[...], w_lo[...]))

    def dense_own():
        sums[:, mine] = dot3((v_hi[...], v_lo[...]), (d_hi[...], d_lo[...]), NT)
        sums[:, theirs] = dot3(
            (v_hi[:, mine], v_lo[:, mine]), (d_hi[:, theirs], d_lo[:, theirs]), NN
        )

    def dense_rest():
        sums[:, theirs] = sums[:, theirs] + dot3(
            (v_hi[:, theirs], v_lo[:, theirs]), (e_hi[...], e_lo[...]), NN
        )

    stages = len(plans[0][-1])

    x_load.wait()
    v_hi[...], v_lo[...] = halves(x_v[...])
    for index, tier in enumerate(reversed(range(tiers))):
        u_loads[tiers - 1 - tier].wait()
        u_hi[tier, :rank], u_lo[tier, :rank] = halves(u_v[tier])
        project(0, tier)
        if index == 0:
            pl.semaphore_wait(barrier, len(near) + 1)
        start(t_copies(0, tier, 0))
        if index == 0:
            e_copy.start()
    d_load.wait()
    d_hi[...], d_lo[...] = halves(d_v[...])
    dense_own()
    c_load.wait()
    c_hi[:, :rank, :rank], c_lo[:, :rank, :rank] = halves(c_v[...])
    for tier in range(low, tiers):
        w_hi[tier - low], w_lo[tier - low] = halves(
            dot3((c_hi[tier], c_lo[tier]), (u_hi[tier], u_lo[tier]), NN)
        )
    for stage in range(stages - 1):
        for tier in reversed(range(first, tiers)):
            if stage + 1 < len(plans[0][tier]):
                forward(0, tier, stage)
        if stage == 0:
            e_copy.wait_recv()
            e_hi[...], e_lo[...] = halves(e_v[...])
            dense_rest()
            b_load.wait()
            base[...] = b_v[...] - sums[...]
            for tier in range(first):
                place(tier, halves(couple(tier, halves(total_of(0, tier)))))
    for tier in range(first, low):
        place(tier, halves(couple(tier, halves(total_of(0, tier)))))
    base[...] = base[...] - spread_low()
    for tier in range(low, tiers):
        place(tier, halves(total_of(0, tier)))
    residual = base[...] - spread_high()
    r_ref[...] = residual
    v_hi[...], v_lo[...] = halves(residual)

    for tier in reversed(range(low, tiers)):
        project(1, tier)
        start(t_copies(1, tier, 0))
    blocks = tuple(part[:low].reshape(low * padded, leaf) for part in (u_hi, u_lo))
    products = dot3((v_hi[...], v_lo[...]), blocks, NT)
    for tier in range(low):
        t_out[1, tier, 0] = pack(products[:, tier * padded : (tier + 1) * padded], rank)
        start(t_copies(1, tier, 0))
    dense_own()
    dense_rest()
    r_now = r_ref[...]
    rows = [row_of(lane_fold(r_now * r_now), lane_fold(r_now * sums[...]))]
    s_out[...] = rows[0]
    start(s_copies())

    def quadratic(tier, total):
        coupled = couple(tier, halves(total))
        found = lane_fold(total * coupled)
        rows.append(row_of(jnp.zeros_like(found), found))
        if tier < tiers - 1:
            q_out[tier] = rows[-1]
            start(q_copies(tier))
        return coupled

    for stage in range(stages - 1):
        for tier in reversed(range(low, tiers)):
            if stage + 1 < len(plans[1][tier]):
                forward(1, tier, stage)
        if stage == 0:
            for tier in range(low):
                place(tier, halves(quadratic(tier, total_of(1, tier))))
            base[...] = sums[...] + spread_low()
    e_copy.wait_send()
    for tier, plan in enumerate(plans[0]):
        for stage in range(len(plan)):
            sent(0, tier, stage)
    for tier, plan in enumerate(plans[1]):
        for stage in range(len(plan) - 1):
            sent(1, tier, stage)
    wait_all(s_in, s_send)
    for tier in range(low, tiers):
        total = total_of(1, tier)
        place(tier, halves(total))
        quadratic(tier, total)
    image_ref[...] = base[...] + spread_high()
    wait_all(s_in, s_recv)
    row = jnp.sum(s_in[...], axis=0)
    for tier in range(tiers - 1):
        into = q_in.at[tier, : len(masks_over(tier + 1, tiers))]
        wait_all(into, q_recv.at[tier])
        row = row + jnp.sum(into[...], axis=0)
    row = row + sum(rows)
    columns = jnp.broadcast_to(row, (row.shape[1], row.shape[1])).T
    step_ref[...] = columns[:cols] / columns[cols:]

    for tier in range(tiers):
        sent(1, tier, len(plans[1][tier]) - 1)
    for tier in range(tiers - 1):
        into = q_in.at[tier, : len(masks_over(tier + 1, tiers))]
        wait_all(into, q_send.at[tier])


def local(rhs_matrix, initial_guess, leaf_blocks, row_bases, couplings):
    tiers, rank, leaf = row_bases.shape
    cols = initial_guess.shape[1]
    half = leaf // 2
    padded = pl.cdiv(rank, LANES) * LANES
    plans = [plan_of(turn, tier) for turn in range(2) for tier in range(tiers)]
    low = sum(len(plan) == 1 for plan in plans[tiers:])
    stages, most = len(plans[-1]), max(len(masks) for plan in plans for masks in plan)
    assert 2 * cols == LANES and leaf_blocks.shape == (half, leaf) and low < tiers
    assert 2**tiers == lax.axis_size("leaf") and lax.axis_size("rhs") == 2
    any_spec = pl.BlockSpec(memory_space=pl.ANY)
    vmem_spec = pl.BlockSpec(memory_space=pltpu.VMEM)
    vmem, dma = pltpu.VMEM, pltpu.SemaphoreType.DMA
    packed = pack_shape(cols, rank)
    guess = initial_guess.T
    residual, image, step = pl.pallas_call(
        kernel,
        out_shape=[vmem((cols, leaf), F32), vmem((cols, leaf), F32), vmem((cols, LANES), F32)],
        in_specs=[any_spec] * 5,
        out_specs=[vmem_spec] * 3,
        scratch_shapes=[
            vmem((cols, leaf), F32),
            vmem((cols, leaf), F32),
            vmem((half, leaf), F32),
            vmem((half, half), F32),
            vmem((tiers, rank, leaf), F32),
            vmem((tiers, rank, rank), F32),
            vmem((half, leaf), BF16),
            vmem((half, leaf), BF16),
            vmem((half, half), BF16),
            vmem((half, half), BF16),
            vmem((tiers, padded, leaf), BF16),
            vmem((tiers, padded, leaf), BF16),
            vmem((tiers, padded, padded), BF16),
            vmem((tiers, padded, padded), BF16),
            vmem((tiers - low, padded, leaf), BF16),
            vmem((tiers - low, padded, leaf), BF16),
            vmem((cols, leaf), BF16),
            vmem((cols, leaf), BF16),
            vmem((cols, tiers * padded), BF16),
            vmem((cols, tiers * padded), BF16),
            vmem((cols, leaf), F32),
            vmem((cols, leaf), F32),
            vmem((2, tiers, stages, *packed), F32),
            vmem((2, tiers, stages, most, *packed), F32),
            vmem((1, LANES), F32),
            vmem((2**tiers - 1, 1, LANES), F32),
            vmem((tiers, 1, LANES), F32),
            vmem((tiers, 2 ** (tiers - 1) - 1, 1, LANES), F32),
            dma((4 + tiers,)),
            dma,
            dma,
            dma((2, tiers, stages)),
            dma((2, tiers, stages)),
            dma,
            dma,
            dma((tiers,)),
            dma((tiers,)),
        ],
        compiler_params=pltpu.CompilerParams(collective_id=0, has_side_effects=True),
        name="cg_step",
    )(guess, rhs_matrix.T, leaf_blocks, row_bases, couplings)
    alpha = jnp.tile(step, (1, leaf // LANES))
    return (guess + alpha * residual).T, (residual - alpha * image).T


def solution(mesh):
    return jax.shard_map(
        local,
        mesh=mesh,
        in_specs=(
            P("leaf", "rhs"),
            P("leaf", "rhs"),
            P(("leaf", "rhs"), None),
            P(None, None, "leaf"),
            P(),
        ),
        out_specs=(P("leaf", "rhs"), P("leaf", "rhs")),
        check_vma=False,
    )
```

```python
import functools

import jax
import jax.numpy as jnp
from jax import lax
from jax.experimental import pallas as pl
from jax.experimental.pallas import tpu as pltpu
from jax.sharding import PartitionSpec as P

MESH = pl.DeviceIdType.MESH
F32 = jnp.float32
BF16 = jnp.bfloat16
LANES = 128
DIRECT = 8
NN = (((1,), (0,)), ((), ()))
NT = (((1,), (1,)), ((), ()))


def halves(value):
    high = value.astype(BF16)
    return high, (value - high.astype(F32)).astype(BF16)


def dot3(left, right, dims):
    rows = left[0].shape[0]
    stacked = lax.dot_general(
        jnp.concatenate(left, axis=0), right[0], dims, preferred_element_type=F32
    )
    cross = lax.dot_general(left[0], right[1], dims, preferred_element_type=F32)
    return stacked[:rows] + (stacked[rows:] + cross)


def lane_fold(value):
    total = value[:, :LANES]
    for start in range(LANES, value.shape[1], LANES):
        total = total + value[:, start : start + LANES]
    return total


def masks_over(low, high):
    return [value << low for value in range(2 ** (high - low) - 1, 0, -1)]


def plan_of(turn, tier):
    if turn == 1 and 2 ** (tier + 1) <= DIRECT:
        return [masks_over(0, tier + 1)]
    return [masks_over(low, min(low + 2, tier + 1)) for low in range(0, tier + 1, 2)]


def flip(leaf_index, mask):
    bit = 1
    while bit <= mask:
        if mask & bit:
            leaf_index = leaf_index + bit * (1 - 2 * ((leaf_index // bit) % 2))
        bit *= 2
    return leaf_index


def pack_shape(cols, rank):
    padded = pl.cdiv(rank, LANES) * LANES
    spare = padded - rank
    if padded != LANES or not spare or rank % spare or cols * spare % (8 * LANES):
        return cols, padded
    return cols * rank // LANES, LANES


def pack(value, rank):
    cols, padded = value.shape
    keep = pack_shape(cols, rank)[0]
    if keep == cols:
        return value
    spare = padded - rank
    extra = value[keep:]
    moved = [
        pltpu.roll(extra, (rank - start) % padded, axis=1) for start in range(0, rank, spare)
    ]
    lane = lax.broadcasted_iota(jnp.int32, (keep, padded), 1)
    return jnp.where(lane < rank, value[:keep], jnp.concatenate(moved, axis=0))


def unpack(value, cols, rank):
    keep, padded = value.shape
    if keep == cols:
        return value
    spare = padded - rank
    count = cols - keep
    lane = lax.broadcasted_iota(jnp.int32, (count, padded), 1)
    extra = jnp.zeros((count, padded), F32)
    for index, start in enumerate(range(0, rank, spare)):
        part = pltpu.roll(
            value[index * count : (index + 1) * count], (start - rank) % padded, axis=1
        )
        extra = jnp.where((lane >= start) & (lane < start + spare), part, extra)
    lane = lax.broadcasted_iota(jnp.int32, (keep, padded), 1)
    return jnp.concatenate([jnp.where(lane < rank, value, 0.0), extra], axis=0)


def row_of(upper, lower):
    stacked = jnp.concatenate([upper, lower], axis=0)
    return jnp.sum(stacked.T, axis=0, keepdims=True)


def kernel(
    x_hbm, b_hbm, d_hbm, u_hbm, c_hbm,
    r_ref, image_ref, step_ref,
    x_v, b_v, d_v, e_v, u_v, c_v,
    d_hi, d_lo, e_hi, e_lo, u_hi, u_lo, c_hi, c_lo, w_hi, w_lo, v_hi, v_lo, cc_hi, cc_lo,
    sums, base, t_out, t_in, s_out, s_in, q_out, q_in,
    local_sem, e_send, e_recv, t_send, t_recv, s_send, s_recv, q_send, q_recv,
):
    tiers, rank, leaf = u_v.shape
    cols = x_v.shape[0]
    half = leaf // 2
    padded = u_hi.shape[1]
    me, core = lax.axis_index("leaf"), lax.axis_index("rhs")
    other = 1 - core
    mine = pl.ds(pl.multiple_of(core * half, half), half)
    theirs = pl.ds(pl.multiple_of(other * half, half), half)
    plans = [[plan_of(turn, tier) for tier in range(tiers)] for turn in range(2)]
    first, low = [sum(len(plan) == 1 for plan in each) for each in plans]
    everyone = masks_over(0, tiers)
    near = [mask for masks in plans[0][-1] for mask in reversed(masks)]

    barrier = pltpu.get_barrier_semaphore()
    for target in [(flip(me, mask), core) for mask in near] + [(me, other)]:
        pl.semaphore_signal(barrier, inc=1, device_id=target, device_id_type=MESH)

    arrays = [(x_hbm, x_v)]
    arrays += [(u_hbm.at[tier], u_v.at[tier]) for tier in reversed(range(tiers))]
    arrays += [(d_hbm, d_v), (c_hbm, c_v), (b_hbm, b_v)]
    loads = [
        pltpu.make_async_copy(source, target, local_sem.at[index])
        for index, (source, target) in enumerate(arrays)
    ]
    for load in loads:
        load.start()
    x_load, *u_loads, d_load, c_load, b_load = loads

    def remote(source, target, send, recv, device):
        return pltpu.make_async_remote_copy(
            src_ref=source, dst_ref=target, send_sem=send, recv_sem=recv,
            device_id=device, device_id_type=MESH,
        )

    e_copy = remote(d_hbm.at[:, mine], e_v, e_send, e_recv, (me, other))

    def t_copies(turn, tier, stage):
        at = (turn, tier, stage)
        return [
            remote(
                t_out.at[at], t_in.at[(*at, index)], t_send.at[at], t_recv.at[at],
                (flip(me, mask), core),
            )
            for index, mask in enumerate(plans[turn][tier][stage])
        ]

    def s_copies():
        return [
            remote(s_out, s_in.at[index], s_send, s_recv, (flip(me, mask), core))
            for index, mask in enumerate(everyone)
        ]

    def q_copies(tier):
        return [
            remote(
                q_out.at[tier], q_in.at[tier, index], q_send.at[tier], q_recv.at[tier],
                (flip(me, mask), core),
            )
            for index, mask in enumerate(masks_over(tier + 1, tiers))
        ]

    def start(copies):
        for copy in copies:
            copy.start()

    def wait_all(buffer, sem):
        pltpu.make_async_copy(buffer, buffer, sem).wait()

    if padded > rank:
        blank = jnp.zeros((tiers, padded - rank, leaf), BF16)
        u_hi[:, rank:, :] = blank
        u_lo[:, rank:, :] = blank
    c_hi[...] = jnp.zeros_like(c_hi)
    c_lo[...] = jnp.zeros_like(c_lo)

    def project(turn, tier):
        products = dot3((v_hi[...], v_lo[...]), (u_hi[tier], u_lo[tier]), NT)
        t_out[turn, tier, 0] = pack(products, rank)

    def gathered(turn, tier, stage):
        count = len(plans[turn][tier][stage])
        into = t_in.at[turn, tier, stage, :count]
        wait_all(into, t_recv.at[turn, tier, stage])
        return t_out[turn, tier, stage] + jnp.sum(into[...], axis=0)

    def sent(turn, tier, stage):
        count = len(plans[turn][tier][stage])
        wait_all(t_in.at[turn, tier, stage, :count], t_send.at[turn, tier, stage])

    def forward(turn, tier, stage):
        t_out[turn, tier, stage + 1] = gathered(turn, tier, stage)
        start(t_copies(turn, tier, stage + 1))

    def total_of(turn, tier):
        return unpack(gathered(turn, tier, len(plans[turn][tier]) - 1), cols, rank)

    def couple(tier, total):
        return dot3(total, (c_hi[tier], c_lo[tier]), NT)

    def place(tier, value):
        at = slice(tier * padded, (tier + 1) * padded)
        cc_hi[:, at], cc_lo[:, at] = value

    def spread(first, last, parts):
        at = slice(first * padded, last * padded)
        count = (last - first) * padded
        return dot3(
            (cc_hi[:, at], cc_lo[:, at]),
            tuple(part.reshape(count, leaf) for part in parts),
            NN,
        )

    def spread_low(last):
        return spread(0, last, (u_hi[:last], u_lo[:last]))

    def spread_high(start_tier):
        return spread(
            start_tier, tiers, (w_hi[start_tier - first :], w_lo[start_tier - first :])
        )

    def dense_own():
        sums[:, mine] = dot3((v_hi[...], v_lo[...]), (d_hi[...], d_lo[...]), NT)
        sums[:, theirs] = dot3(
            (v_hi[:, mine], v_lo[:, mine]), (d_hi[:, theirs], d_lo[:, theirs]), NN
        )

    def dense_rest():
        sums[:, theirs] = sums[:, theirs] + dot3(
            (v_hi[:, theirs], v_lo[:, theirs]), (e_hi[...], e_lo[...]), NN
        )

    stages = len(plans[0][-1])

    x_load.wait()
    v_hi[...], v_lo[...] = halves(x_v[...])
    for index, tier in enumerate(reversed(range(tiers))):
        u_loads[tiers - 1 - tier].wait()
        u_hi[tier, :rank], u_lo[tier, :rank] = halves(u_v[tier])
        project(0, tier)
        if index == 0:
            pl.semaphore_wait(barrier, len(near) + 1)
        start(t_copies(0, tier, 0))
        if index == 0:
            e_copy.start()
    d_load.wait()
    d_hi[...], d_lo[...] = halves(d_v[...])
    dense_own()
    c_load.wait()
    c_hi[:, :rank, :rank], c_lo[:, :rank, :rank] = halves(c_v[...])
    for tier in range(first, tiers):
        w_hi[tier - first], w_lo[tier - first] = halves(
            dot3((c_hi[tier], c_lo[tier]), (u_hi[tier], u_lo[tier]), NN)
        )
    for stage in range(stages - 1):
        for tier in reversed(range(first, tiers)):
            if stage + 1 < len(plans[0][tier]):
                forward(0, tier, stage)
        if stage == 0:
            e_copy.wait_recv()
            e_hi[...], e_lo[...] = halves(e_v[...])
            dense_rest()
            b_load.wait()
            base[...] = b_v[...] - sums[...]
            for tier in range(first):
                place(tier, halves(couple(tier, halves(total_of(0, tier)))))
            base[...] = base[...] - spread_low(first)
    for tier in range(first, tiers):
        place(tier, halves(total_of(0, tier)))
    residual = base[...] - spread_high(first)
    r_ref[...] = residual
    v_hi[...], v_lo[...] = halves(residual)

    for tier in reversed(range(low, tiers)):
        project(1, tier)
        start(t_copies(1, tier, 0))
    blocks = tuple(part[:low].reshape(low * padded, leaf) for part in (u_hi, u_lo))
    products = dot3((v_hi[...], v_lo[...]), blocks, NT)
    for tier in range(low):
        t_out[1, tier, 0] = pack(products[:, tier * padded : (tier + 1) * padded], rank)
        start(t_copies(1, tier, 0))
    dense_own()
    dense_rest()
    r_now = r_ref[...]
    rows = [row_of(lane_fold(r_now * r_now), lane_fold(r_now * sums[...]))]
    s_out[...] = rows[0]
    start(s_copies())

    def quadratic(tier, total):
        coupled = couple(tier, halves(total))
        found = lane_fold(total * coupled)
        rows.append(row_of(jnp.zeros_like(found), found))
        if tier < tiers - 1:
            q_out[tier] = rows[-1]
            start(q_copies(tier))
        return coupled

    for stage in range(stages - 1):
        for tier in reversed(range(low, tiers)):
            if stage + 1 < len(plans[1][tier]):
                forward(1, tier, stage)
        if stage == 0:
            for tier in range(low):
                place(tier, halves(quadratic(tier, total_of(1, tier))))
            base[...] = sums[...] + spread_low(low)
    e_copy.wait_send()
    for tier, plan in enumerate(plans[0]):
        for stage in range(len(plan)):
            sent(0, tier, stage)
    for tier, plan in enumerate(plans[1]):
        for stage in range(len(plan) - 1):
            sent(1, tier, stage)
    wait_all(s_in, s_send)
    for tier in range(low, tiers):
        total = total_of(1, tier)
        place(tier, halves(total))
        quadratic(tier, total)
    image_ref[...] = base[...] + spread_high(low)
    wait_all(s_in, s_recv)
    row = jnp.sum(s_in[...], axis=0)
    for tier in range(tiers - 1):
        into = q_in.at[tier, : len(masks_over(tier + 1, tiers))]
        wait_all(into, q_recv.at[tier])
        row = row + jnp.sum(into[...], axis=0)
    row = row + sum(rows)
    columns = jnp.broadcast_to(row, (row.shape[1], row.shape[1])).T
    step_ref[...] = columns[:cols] / columns[cols:]

    for tier in range(tiers):
        sent(1, tier, len(plans[1][tier]) - 1)
    for tier in range(tiers - 1):
        into = q_in.at[tier, : len(masks_over(tier + 1, tiers))]
        wait_all(into, q_send.at[tier])


def local(rhs_matrix, initial_guess, leaf_blocks, row_bases, couplings):
    tiers, rank, leaf = row_bases.shape
    cols = initial_guess.shape[1]
    half = leaf // 2
    padded = pl.cdiv(rank, LANES) * LANES
    plans = [plan_of(turn, tier) for turn in range(2) for tier in range(tiers)]
    first, low = [sum(len(plan) == 1 for plan in each) for each in (plans[:tiers], plans[tiers:])]
    stages, most = len(plans[-1]), max(len(masks) for plan in plans for masks in plan)
    assert 2 * cols == LANES and leaf_blocks.shape == (half, leaf) and low < tiers
    assert 2**tiers == lax.axis_size("leaf") and lax.axis_size("rhs") == 2
    any_spec = pl.BlockSpec(memory_space=pl.ANY)
    vmem_spec = pl.BlockSpec(memory_space=pltpu.VMEM)
    vmem, dma = pltpu.VMEM, pltpu.SemaphoreType.DMA
    packed = pack_shape(cols, rank)
    guess = initial_guess.T
    residual, image, step = pl.pallas_call(
        kernel,
        out_shape=[vmem((cols, leaf), F32), vmem((cols, leaf), F32), vmem((cols, LANES), F32)],
        in_specs=[any_spec] * 5,
        out_specs=[vmem_spec] * 3,
        scratch_shapes=[
            vmem((cols, leaf), F32),
            vmem((cols, leaf), F32),
            vmem((half, leaf), F32),
            vmem((half, half), F32),
            vmem((tiers, rank, leaf), F32),
            vmem((tiers, rank, rank), F32),
            vmem((half, leaf), BF16),
            vmem((half, leaf), BF16),
            vmem((half, half), BF16),
            vmem((half, half), BF16),
            vmem((tiers, padded, leaf), BF16),
            vmem((tiers, padded, leaf), BF16),
            vmem((tiers, padded, padded), BF16),
            vmem((tiers, padded, padded), BF16),
            vmem((tiers - first, padded, leaf), BF16),
            vmem((tiers - first, padded, leaf), BF16),
            vmem((cols, leaf), BF16),
            vmem((cols, leaf), BF16),
            vmem((cols, tiers * padded), BF16),
            vmem((cols, tiers * padded), BF16),
            vmem((cols, leaf), F32),
            vmem((cols, leaf), F32),
            vmem((2, tiers, stages, *packed), F32),
            vmem((2, tiers, stages, most, *packed), F32),
            vmem((1, LANES), F32),
            vmem((2**tiers - 1, 1, LANES), F32),
            vmem((tiers, 1, LANES), F32),
            vmem((tiers, 2 ** (tiers - 1) - 1, 1, LANES), F32),
            dma((4 + tiers,)),
            dma,
            dma,
            dma((2, tiers, stages)),
            dma((2, tiers, stages)),
            dma,
            dma,
            dma((tiers,)),
            dma((tiers,)),
        ],
        compiler_params=pltpu.CompilerParams(collective_id=0, has_side_effects=True),
        name="cg_step",
    )(guess, rhs_matrix.T, leaf_blocks, row_bases, couplings)
    alpha = jnp.tile(step, (1, leaf // LANES))
    return (guess + alpha * residual).T, (residual - alpha * image).T


def solution(mesh):
    return jax.shard_map(
        local,
        mesh=mesh,
        in_specs=(
            P("leaf", "rhs"),
            P("leaf", "rhs"),
            P(("leaf", "rhs"), None),
            P(None, None, "leaf"),
            P(),
        ),
        out_specs=(P("leaf", "rhs"), P("leaf", "rhs")),
        check_vma=False,
    )
```

```python
import functools

import jax
import jax.numpy as jnp
from jax import lax
from jax.experimental import pallas as pl
from jax.experimental.pallas import tpu as pltpu
from jax.sharding import PartitionSpec as P

MESH = pl.DeviceIdType.MESH
F32 = jnp.float32
BF16 = jnp.bfloat16
LANES = 128
DIRECT = 8
NN = (((1,), (0,)), ((), ()))
NT = (((1,), (1,)), ((), ()))


def halves(value):
    high = value.astype(BF16)
    return high, (value - high.astype(F32)).astype(BF16)


def dot3(left, right, dims):
    rows = left[0].shape[0]
    stacked = lax.dot_general(
        jnp.concatenate(left, axis=0), right[0], dims, preferred_element_type=F32
    )
    cross = lax.dot_general(left[0], right[1], dims, preferred_element_type=F32)
    return stacked[:rows] + (stacked[rows:] + cross)


def lane_fold(value):
    total = value[:, :LANES]
    for start in range(LANES, value.shape[1], LANES):
        total = total + value[:, start : start + LANES]
    return total


def masks_over(low, high):
    return [value << low for value in range(2 ** (high - low) - 1, 0, -1)]


def plan_of(turn, tier):
    if turn == 1 and 2 ** (tier + 1) <= DIRECT:
        return [masks_over(0, tier + 1)]
    return [masks_over(low, min(low + 2, tier + 1)) for low in range(0, tier + 1, 2)]


def layout_of(plans):
    slots, counts = {}, []
    for turn, each in enumerate(plans):
        start_slot = sum(counts)
        total = start_slot
        for tier, plan in enumerate(each):
            for stage, masks in enumerate(plan):
                slots[turn, tier, stage] = total
                total += len(masks)
        counts.append(total - start_slot)
    return slots, counts


def row_layout(tiers):
    places, total = [], 2**tiers - 1
    for tier in range(tiers - 1):
        places.append(total)
        total += 2 ** (tiers - 1 - tier) - 1
    return places, total


def flip(leaf_index, mask):
    bit = 1
    while bit <= mask:
        if mask & bit:
            leaf_index = leaf_index + bit * (1 - 2 * ((leaf_index // bit) % 2))
        bit *= 2
    return leaf_index


def pack_shape(cols, rank):
    padded = pl.cdiv(rank, LANES) * LANES
    spare = padded - rank
    if padded != LANES or not spare or rank % spare or cols * spare % (8 * LANES):
        return cols, padded
    return cols * rank // LANES, LANES


def pack(value, rank):
    cols, padded = value.shape
    keep = pack_shape(cols, rank)[0]
    if keep == cols:
        return value
    spare = padded - rank
    extra = value[keep:]
    moved = [
        pltpu.roll(extra, (rank - start) % padded, axis=1) for start in range(0, rank, spare)
    ]
    lane = lax.broadcasted_iota(jnp.int32, (keep, padded), 1)
    return jnp.where(lane < rank, value[:keep], jnp.concatenate(moved, axis=0))


def unpack(value, cols, rank):
    keep, padded = value.shape
    if keep == cols:
        return value
    spare = padded - rank
    count = cols - keep
    lane = lax.broadcasted_iota(jnp.int32, (count, padded), 1)
    extra = jnp.zeros((count, padded), F32)
    for index, start in enumerate(range(0, rank, spare)):
        part = pltpu.roll(
            value[index * count : (index + 1) * count], (start - rank) % padded, axis=1
        )
        extra = jnp.where((lane >= start) & (lane < start + spare), part, extra)
    lane = lax.broadcasted_iota(jnp.int32, (keep, padded), 1)
    return jnp.concatenate([jnp.where(lane < rank, value, 0.0), extra], axis=0)


def row_of(upper, lower):
    stacked = jnp.concatenate([upper, lower], axis=0)
    return jnp.sum(stacked.T, axis=0, keepdims=True)


def kernel(
    x_hbm, b_hbm, d_hbm, u_hbm, c_hbm,
    r_ref, image_ref, step_ref,
    x_v, b_v, d_v, e_v, u_v, c_v,
    d_hi, d_lo, e_hi, e_lo, u_hi, u_lo, c_hi, c_lo, w_hi, w_lo, v_hi, v_lo, cc_hi, cc_lo,
    m_hi, m_lo, early, sums, base, t_out, t_in, row_out, row_in,
    local_sem, e_send, e_recv, t_send, t_recv, row_send, row_recv,
):
    tiers, rank, leaf = u_v.shape
    cols = x_v.shape[0]
    half = leaf // 2
    padded = u_hi.shape[1]
    me, core = lax.axis_index("leaf"), lax.axis_index("rhs")
    other = 1 - core
    mine = pl.ds(pl.multiple_of(core * half, half), half)
    theirs = pl.ds(pl.multiple_of(other * half, half), half)
    plans = [[plan_of(turn, tier) for tier in range(tiers)] for turn in range(2)]
    first, low = [sum(len(plan) == 1 for plan in each) for each in plans]
    everyone = masks_over(0, tiers)
    slots, counts = layout_of(plans)
    gates = {key: index for index, key in enumerate(slots)}
    places, _ = row_layout(tiers)
    near = [mask for masks in plans[0][-1] for mask in reversed(masks)]

    barrier = pltpu.get_barrier_semaphore()
    for target in [(flip(me, mask), core) for mask in near] + [(me, other)]:
        pl.semaphore_signal(barrier, inc=1, device_id=target, device_id_type=MESH)

    arrays = [(x_hbm, x_v)]
    arrays += [(u_hbm.at[part], u_v.at[part]) for part in (slice(tiers - 1, tiers), slice(0, tiers - 1))]
    arrays += [(d_hbm, d_v), (c_hbm, c_v), (b_hbm, b_v)]
    loads = [
        pltpu.make_async_copy(source, target, local_sem.at[index])
        for index, (source, target) in enumerate(arrays)
    ]
    for load in loads:
        load.start()
    x_load, *u_loads, d_load, c_load, b_load = loads

    def remote(source, target, send, recv, device):
        return pltpu.make_async_remote_copy(
            src_ref=source, dst_ref=target, send_sem=send, recv_sem=recv,
            device_id=device, device_id_type=MESH,
        )

    e_copy = remote(d_hbm.at[:, mine], e_v, e_send, e_recv, (me, other))

    def t_copies(turn, tier, stage):
        key = (turn, tier, stage)
        return [
            remote(
                t_out.at[gates[key]], t_in.at[slots[key] + index],
                t_send.at[turn], t_recv.at[gates[key]], (flip(me, mask), core),
            )
            for index, mask in enumerate(plans[turn][tier][stage])
        ]

    def s_copies():
        return [
            remote(row_out.at[tiers - 1], row_in.at[index], row_send, row_recv, (flip(me, mask), core))
            for index, mask in enumerate(everyone)
        ]

    def q_copies(tier):
        return [
            remote(
                row_out.at[tier], row_in.at[places[tier] + index], row_send, row_recv,
                (flip(me, mask), core),
            )
            for index, mask in enumerate(masks_over(tier + 1, tiers))
        ]

    def start(copies):
        for copy in copies:
            copy.start()

    def wait_all(buffer, sem):
        pltpu.make_async_copy(buffer, buffer, sem).wait()

    if padded > rank:
        blank = jnp.zeros((tiers, padded - rank, leaf), BF16)
        u_hi[:, rank:, :] = blank
        u_lo[:, rank:, :] = blank
    c_hi[...] = jnp.zeros_like(c_hi)
    c_lo[...] = jnp.zeros_like(c_lo)

    def project(turn, tier):
        products = dot3((v_hi[...], v_lo[...]), (u_hi[tier], u_lo[tier]), NT)
        t_out[gates[turn, tier, 0]] = pack(products, rank)

    def gathered(turn, tier, stage):
        key = (turn, tier, stage)
        into = t_in.at[slots[key] : slots[key] + len(plans[turn][tier][stage])]
        wait_all(into, t_recv.at[gates[key]])
        return t_out[gates[key]] + jnp.sum(into[...], axis=0)

    def forward(turn, tier, stage):
        t_out[gates[turn, tier, stage + 1]] = gathered(turn, tier, stage)
        start(t_copies(turn, tier, stage + 1))

    def total_of(turn, tier):
        return unpack(gathered(turn, tier, len(plans[turn][tier]) - 1), cols, rank)

    def couple(tier, total):
        return dot3(total, (c_hi[tier], c_lo[tier]), NT)

    def place(tier, value):
        at = slice(tier * padded, (tier + 1) * padded)
        cc_hi[:, at], cc_lo[:, at] = value

    def spread(first, last, parts):
        at = slice(first * padded, last * padded)
        count = (last - first) * padded
        return dot3(
            (cc_hi[:, at], cc_lo[:, at]),
            tuple(part.reshape(count, leaf) for part in parts),
            NN,
        )

    def spread_low(last):
        return spread(0, last, (u_hi[:last], u_lo[:last]))

    def spread_high(start_tier):
        return spread(
            start_tier, tiers, (w_hi[start_tier - first :], w_lo[start_tier - first :])
        )

    def dense_own():
        sums[:, mine] = dot3((v_hi[...], v_lo[...]), (d_hi[...], d_lo[...]), NT)
        sums[:, theirs] = dot3(
            (v_hi[:, mine], v_lo[:, mine]), (d_hi[:, theirs], d_lo[:, theirs]), NN
        )

    def dense_rest():
        sums[:, theirs] = sums[:, theirs] + dot3(
            (v_hi[:, theirs], v_lo[:, theirs]), (e_hi[...], e_lo[...]), NN
        )

    stages = len(plans[0][-1])

    x_load.wait()
    v_hi[...], v_lo[...] = halves(x_v[...])
    for index, tier in enumerate(reversed(range(tiers))):
        if index < 2:
            u_loads[index].wait()
        u_hi[tier, :rank], u_lo[tier, :rank] = halves(u_v[tier])
        project(0, tier)
        if index == 0:
            pl.semaphore_wait(barrier, len(near) + 1)
        start(t_copies(0, tier, 0))
        if index == 0:
            e_copy.start()
    d_load.wait()
    d_hi[...], d_lo[...] = halves(d_v[...])
    dense_own()
    c_load.wait()
    c_hi[:, :rank, :rank], c_lo[:, :rank, :rank] = halves(c_v[...])
    for tier in range(first, tiers):
        w_hi[tier - first], w_lo[tier - first] = halves(
            dot3((c_hi[tier], c_lo[tier]), (u_hi[tier], u_lo[tier]), NN)
        )
    every = tuple(part[...].reshape(tiers * padded, leaf) for part in (u_hi, u_lo))
    for stage in range(stages - 1):
        for tier in reversed(range(first, tiers)):
            if stage + 1 < len(plans[0][tier]):
                forward(0, tier, stage)
        if stage == 0:
            e_copy.wait_recv()
            e_hi[...], e_lo[...] = halves(e_v[...])
            dense_rest()
            b_load.wait()
            base[...] = b_v[...] - sums[...]
            for tier in range(first):
                place(tier, halves(couple(tier, halves(total_of(0, tier)))))
            base[...] = base[...] - spread_low(first)
            early[...] = dot3(halves(base[...]), every, NT)
            count = (tiers - first) * padded
            spreads = tuple(part[...].reshape(count, leaf) for part in (w_hi, w_lo))
            m_hi[...], m_lo[...] = halves(dot3(spreads, every, NT))
    for tier in range(first, tiers):
        place(tier, halves(total_of(0, tier)))
    late = slice(first * padded, tiers * padded)
    products = early[...] - dot3((cc_hi[:, late], cc_lo[:, late]), (m_hi[...], m_lo[...]), NN)
    for tier in [*reversed(range(low, tiers)), *range(low)]:
        t_out[gates[1, tier, 0]] = pack(products[:, tier * padded : (tier + 1) * padded], rank)
        start(t_copies(1, tier, 0))
    residual = base[...] - spread_high(first)
    r_ref[...] = residual
    v_hi[...], v_lo[...] = halves(residual)
    dense_own()
    dense_rest()
    r_now = r_ref[...]
    rows = [row_of(lane_fold(r_now * r_now), lane_fold(r_now * sums[...]))]
    row_out[tiers - 1] = rows[0]
    start(s_copies())

    def quadratic(tier, total):
        coupled = couple(tier, halves(total))
        found = lane_fold(total * coupled)
        rows.append(row_of(jnp.zeros_like(found), found))
        if tier < tiers - 1:
            row_out[tier] = rows[-1]
            start(q_copies(tier))
        return coupled

    for stage in range(stages - 1):
        for tier in reversed(range(low, tiers)):
            if stage + 1 < len(plans[1][tier]):
                forward(1, tier, stage)
        if stage == 0:
            for tier in range(low):
                place(tier, halves(quadratic(tier, total_of(1, tier))))
            base[...] = sums[...] + spread_low(low)
    e_copy.wait_send()
    wait_all(t_in.at[: counts[0]], t_send.at[0])
    for tier in range(low, tiers):
        total = total_of(1, tier)
        place(tier, halves(total))
        quadratic(tier, total)
    image_ref[...] = base[...] + spread_high(low)
    wait_all(row_in, row_recv)
    row = jnp.sum(row_in[...], axis=0) + sum(rows)
    columns = jnp.broadcast_to(row, (row.shape[1], row.shape[1])).T
    step_ref[...] = columns[:cols] / columns[cols:]

    wait_all(t_in.at[counts[0] :], t_send.at[1])
    wait_all(row_in, row_send)


def local(rhs_matrix, initial_guess, leaf_blocks, row_bases, couplings):
    tiers, rank, leaf = row_bases.shape
    cols = initial_guess.shape[1]
    half = leaf // 2
    padded = pl.cdiv(rank, LANES) * LANES
    plans = [[plan_of(turn, tier) for tier in range(tiers)] for turn in range(2)]
    first, low = [sum(len(plan) == 1 for plan in each) for each in plans]
    slots, counts = layout_of(plans)
    row_count = row_layout(tiers)[1]
    assert 2 * cols == LANES and leaf_blocks.shape == (half, leaf) and low < tiers
    assert 2**tiers == lax.axis_size("leaf") and lax.axis_size("rhs") == 2
    any_spec = pl.BlockSpec(memory_space=pl.ANY)
    vmem_spec = pl.BlockSpec(memory_space=pltpu.VMEM)
    vmem, dma = pltpu.VMEM, pltpu.SemaphoreType.DMA
    packed = pack_shape(cols, rank)
    guess = initial_guess.T
    residual, image, step = pl.pallas_call(
        kernel,
        out_shape=[vmem((cols, leaf), F32), vmem((cols, leaf), F32), vmem((cols, LANES), F32)],
        in_specs=[any_spec] * 5,
        out_specs=[vmem_spec] * 3,
        scratch_shapes=[
            vmem((cols, leaf), F32),
            vmem((cols, leaf), F32),
            vmem((half, leaf), F32),
            vmem((half, half), F32),
            vmem((tiers, rank, leaf), F32),
            vmem((tiers, rank, rank), F32),
            vmem((half, leaf), BF16),
            vmem((half, leaf), BF16),
            vmem((half, half), BF16),
            vmem((half, half), BF16),
            vmem((tiers, padded, leaf), BF16),
            vmem((tiers, padded, leaf), BF16),
            vmem((tiers, padded, padded), BF16),
            vmem((tiers, padded, padded), BF16),
            vmem((tiers - first, padded, leaf), BF16),
            vmem((tiers - first, padded, leaf), BF16),
            vmem((cols, leaf), BF16),
            vmem((cols, leaf), BF16),
            vmem((cols, tiers * padded), BF16),
            vmem((cols, tiers * padded), BF16),
            vmem(((tiers - first) * padded, tiers * padded), BF16),
            vmem(((tiers - first) * padded, tiers * padded), BF16),
            vmem((cols, tiers * padded), F32),
            vmem((cols, leaf), F32),
            vmem((cols, leaf), F32),
            vmem((len(slots), *packed), F32),
            vmem((sum(counts), *packed), F32),
            vmem((tiers, 1, LANES), F32),
            vmem((row_count, 1, LANES), F32),
            dma((6,)),
            dma,
            dma,
            dma((2,)),
            dma((len(slots),)),
            dma,
            dma,
        ],
        compiler_params=pltpu.CompilerParams(collective_id=0, has_side_effects=True),
        name="cg_step",
    )(guess, rhs_matrix.T, leaf_blocks, row_bases, couplings)
    alpha = jnp.tile(step, (1, leaf // LANES))
    return (guess + alpha * residual).T, (residual - alpha * image).T


def solution(mesh):
    return jax.shard_map(
        local,
        mesh=mesh,
        in_specs=(
            P("leaf", "rhs"),
            P("leaf", "rhs"),
            P(("leaf", "rhs"), None),
            P(None, None, "leaf"),
            P(),
        ),
        out_specs=(P("leaf", "rhs"), P("leaf", "rhs")),
        check_vma=False,
    )
```

```python
import functools

import jax
import jax.numpy as jnp
from jax import lax
from jax.experimental import pallas as pl
from jax.experimental.pallas import tpu as pltpu
from jax.sharding import PartitionSpec as P

MESH = pl.DeviceIdType.MESH
F32 = jnp.float32
BF16 = jnp.bfloat16
LANES = 128
DIRECT = 8
NN = (((1,), (0,)), ((), ()))
NT = (((1,), (1,)), ((), ()))


def halves(value):
    high = value.astype(BF16)
    return high, (value - high.astype(F32)).astype(BF16)


def dot3(left, right, dims):
    rows = left[0].shape[0]
    stacked = lax.dot_general(
        jnp.concatenate(left, axis=0), right[0], dims, preferred_element_type=F32
    )
    cross = lax.dot_general(left[0], right[1], dims, preferred_element_type=F32)
    return stacked[:rows] + (stacked[rows:] + cross)


def lane_fold(value):
    total = value[:, :LANES]
    for start in range(LANES, value.shape[1], LANES):
        total = total + value[:, start : start + LANES]
    return total


def masks_over(low, high):
    return [value << low for value in range(2 ** (high - low) - 1, 0, -1)]


def plan_of(turn, tier):
    if turn == 1 and 2 ** (tier + 1) <= DIRECT:
        return [masks_over(0, tier + 1)]
    return [masks_over(low, min(low + 2, tier + 1)) for low in range(0, tier + 1, 2)]


def layout_of(plans):
    slots, counts = {}, []
    for turn, each in enumerate(plans):
        start_slot = sum(counts)
        total = start_slot
        for tier, plan in enumerate(each):
            for stage, masks in enumerate(plan):
                slots[turn, tier, stage] = total
                total += len(masks)
        counts.append(total - start_slot)
    return slots, counts


def row_layout(tiers):
    places, total = [], 2**tiers - 1
    for tier in range(tiers - 1):
        places.append(total)
        total += 2 ** (tiers - 1 - tier) - 1
    return places, total


def flip(leaf_index, mask):
    bit = 1
    while bit <= mask:
        if mask & bit:
            leaf_index = leaf_index + bit * (1 - 2 * ((leaf_index // bit) % 2))
        bit *= 2
    return leaf_index


def pack_shape(cols, rank):
    padded = pl.cdiv(rank, LANES) * LANES
    spare = padded - rank
    if padded != LANES or not spare or rank % spare or cols * spare % (8 * LANES):
        return cols, padded
    return cols * rank // LANES, LANES


def pack(value, rank):
    cols, padded = value.shape
    keep = pack_shape(cols, rank)[0]
    if keep == cols:
        return value
    spare = padded - rank
    extra = value[keep:]
    moved = [
        pltpu.roll(extra, (rank - start) % padded, axis=1) for start in range(0, rank, spare)
    ]
    lane = lax.broadcasted_iota(jnp.int32, (keep, padded), 1)
    return jnp.where(lane < rank, value[:keep], jnp.concatenate(moved, axis=0))


def unpack(value, cols, rank):
    keep, padded = value.shape
    if keep == cols:
        return value
    spare = padded - rank
    count = cols - keep
    lane = lax.broadcasted_iota(jnp.int32, (count, padded), 1)
    extra = jnp.zeros((count, padded), F32)
    for index, start in enumerate(range(0, rank, spare)):
        part = pltpu.roll(
            value[index * count : (index + 1) * count], (start - rank) % padded, axis=1
        )
        extra = jnp.where((lane >= start) & (lane < start + spare), part, extra)
    lane = lax.broadcasted_iota(jnp.int32, (keep, padded), 1)
    return jnp.concatenate([jnp.where(lane < rank, value, 0.0), extra], axis=0)


def row_of(upper, lower):
    stacked = jnp.concatenate([upper, lower], axis=0)
    return jnp.sum(stacked.T, axis=0, keepdims=True)


def kernel(
    x_hbm, b_hbm, d_hbm, u_hbm, c_hbm,
    r_ref, image_ref, step_ref, x_v,
    b_v, d_v, e_v, u_v, c_v,
    d_hi, d_lo, e_hi, e_lo, u_hi, u_lo, c_hi, c_lo, w_hi, w_lo, v_hi, v_lo, cc_hi, cc_lo,
    m_hi, m_lo, early, sums, base, t_out, t_in, row_out, row_in,
    local_sem, e_send, e_recv, t_send, t_recv, row_send, row_recv,
):
    tiers, rank, leaf = u_v.shape
    cols = x_v.shape[0]
    half = leaf // 2
    padded = u_hi.shape[1]
    me, core = lax.axis_index("leaf"), lax.axis_index("rhs")
    other = 1 - core
    mine = pl.ds(pl.multiple_of(core * half, half), half)
    theirs = pl.ds(pl.multiple_of(other * half, half), half)
    plans = [[plan_of(turn, tier) for tier in range(tiers)] for turn in range(2)]
    first, low = [sum(len(plan) == 1 for plan in each) for each in plans]
    everyone = masks_over(0, tiers)
    slots, counts = layout_of(plans)
    gates = {key: index for index, key in enumerate(slots)}
    places, _ = row_layout(tiers)
    near = [mask for masks in plans[0][-1] for mask in reversed(masks)]

    barrier = pltpu.get_barrier_semaphore()
    for target in [(flip(me, mask), core) for mask in near] + [(me, other)]:
        pl.semaphore_signal(barrier, inc=1, device_id=target, device_id_type=MESH)

    arrays = [(x_hbm, x_v)]
    arrays += [(u_hbm.at[part], u_v.at[part]) for part in (slice(tiers - 1, tiers), slice(0, tiers - 1))]
    arrays += [(d_hbm, d_v), (c_hbm, c_v), (b_hbm, b_v)]
    loads = [
        pltpu.make_async_copy(source, target, local_sem.at[index])
        for index, (source, target) in enumerate(arrays)
    ]
    for load in loads:
        load.start()
    x_load, *u_loads, d_load, c_load, b_load = loads

    def remote(source, target, send, recv, device):
        return pltpu.make_async_remote_copy(
            src_ref=source, dst_ref=target, send_sem=send, recv_sem=recv,
            device_id=device, device_id_type=MESH,
        )

    e_copy = remote(d_hbm.at[:, mine], e_v, e_send, e_recv, (me, other))

    def t_copies(turn, tier, stage):
        key = (turn, tier, stage)
        return [
            remote(
                t_out.at[gates[key]], t_in.at[slots[key] + index],
                t_send, t_recv.at[gates[key]], (flip(me, mask), core),
            )
            for index, mask in enumerate(plans[turn][tier][stage])
        ]

    def s_copies():
        return [
            remote(row_out.at[tiers - 1], row_in.at[index], row_send, row_recv, (flip(me, mask), core))
            for index, mask in enumerate(everyone)
        ]

    def q_copies(tier):
        return [
            remote(
                row_out.at[tier], row_in.at[places[tier] + index], row_send, row_recv,
                (flip(me, mask), core),
            )
            for index, mask in enumerate(masks_over(tier + 1, tiers))
        ]

    def start(copies):
        for copy in copies:
            copy.start()

    def wait_all(buffer, sem):
        pltpu.make_async_copy(buffer, buffer, sem).wait()

    if padded > rank:
        blank = jnp.zeros((tiers, padded - rank, leaf), BF16)
        u_hi[:, rank:, :] = blank
        u_lo[:, rank:, :] = blank
    c_hi[...] = jnp.zeros_like(c_hi)
    c_lo[...] = jnp.zeros_like(c_lo)

    def project(turn, tier):
        products = dot3((v_hi[...], v_lo[...]), (u_hi[tier], u_lo[tier]), NT)
        t_out[gates[turn, tier, 0]] = pack(products, rank)

    def gathered(turn, tier, stage):
        key = (turn, tier, stage)
        into = t_in.at[slots[key] : slots[key] + len(plans[turn][tier][stage])]
        wait_all(into, t_recv.at[gates[key]])
        return t_out[gates[key]] + jnp.sum(into[...], axis=0)

    def forward(turn, tier, stage):
        t_out[gates[turn, tier, stage + 1]] = gathered(turn, tier, stage)
        start(t_copies(turn, tier, stage + 1))

    def total_of(turn, tier):
        return unpack(gathered(turn, tier, len(plans[turn][tier]) - 1), cols, rank)

    def couple(tier, total):
        return dot3(total, (c_hi[tier], c_lo[tier]), NT)

    def place(tier, value):
        at = slice(tier * padded, (tier + 1) * padded)
        cc_hi[:, at], cc_lo[:, at] = value

    def spread(first, last, parts):
        at = slice(first * padded, last * padded)
        count = (last - first) * padded
        return dot3(
            (cc_hi[:, at], cc_lo[:, at]),
            tuple(part.reshape(count, leaf) for part in parts),
            NN,
        )

    def spread_low(last):
        return spread(0, last, (u_hi[:last], u_lo[:last]))

    def spread_high(start_tier):
        return spread(
            start_tier, tiers, (w_hi[start_tier - first :], w_lo[start_tier - first :])
        )

    def dense_own():
        sums[:, mine] = dot3((v_hi[...], v_lo[...]), (d_hi[...], d_lo[...]), NT)
        sums[:, theirs] = dot3(
            (v_hi[:, mine], v_lo[:, mine]), (d_hi[:, theirs], d_lo[:, theirs]), NN
        )

    def dense_rest():
        sums[:, theirs] = sums[:, theirs] + dot3(
            (v_hi[:, theirs], v_lo[:, theirs]), (e_hi[...], e_lo[...]), NN
        )

    stages = len(plans[0][-1])

    x_load.wait()
    v_hi[...], v_lo[...] = halves(x_v[...])
    for index, tier in enumerate(reversed(range(tiers))):
        if index < 2:
            u_loads[index].wait()
        u_hi[tier, :rank], u_lo[tier, :rank] = halves(u_v[tier])
        project(0, tier)
        if index == 0:
            pl.semaphore_wait(barrier, len(near) + 1)
        start(t_copies(0, tier, 0))
        if index == 0:
            e_copy.start()
    d_load.wait()
    d_hi[...], d_lo[...] = halves(d_v[...])
    dense_own()
    c_load.wait()
    c_hi[:, :rank, :rank], c_lo[:, :rank, :rank] = halves(c_v[...])
    for tier in range(first, tiers):
        w_hi[tier - first], w_lo[tier - first] = halves(
            dot3((c_hi[tier], c_lo[tier]), (u_hi[tier], u_lo[tier]), NN)
        )
    every = tuple(part[...].reshape(tiers * padded, leaf) for part in (u_hi, u_lo))
    for stage in range(stages - 1):
        for tier in reversed(range(first, tiers)):
            if stage + 1 < len(plans[0][tier]):
                forward(0, tier, stage)
        if stage == 0:
            e_copy.wait_recv()
            e_hi[...], e_lo[...] = halves(e_v[...])
            dense_rest()
            b_load.wait()
            base[...] = b_v[...] - sums[...]
            for tier in range(first):
                place(tier, halves(couple(tier, halves(total_of(0, tier)))))
            base[...] = base[...] - spread_low(first)
            early[...] = dot3(halves(base[...]), every, NT)
            count = (tiers - first) * padded
            spreads = tuple(part[...].reshape(count, leaf) for part in (w_hi, w_lo))
            m_hi[...], m_lo[...] = halves(dot3(spreads, every, NT))
    for tier in range(first, tiers):
        place(tier, halves(total_of(0, tier)))
    late = slice(first * padded, tiers * padded)
    products = early[...] - dot3((cc_hi[:, late], cc_lo[:, late]), (m_hi[...], m_lo[...]), NN)
    for tier in [*reversed(range(low, tiers)), *range(low)]:
        t_out[gates[1, tier, 0]] = pack(products[:, tier * padded : (tier + 1) * padded], rank)
        start(t_copies(1, tier, 0))
    residual = base[...] - spread_high(first)
    r_ref[...] = residual
    v_hi[...], v_lo[...] = halves(residual)
    dense_own()
    dense_rest()
    r_now = r_ref[...]
    rows = [row_of(lane_fold(r_now * r_now), lane_fold(r_now * sums[...]))]
    row_out[tiers - 1] = rows[0]
    start(s_copies())

    def quadratic(tier, total):
        coupled = couple(tier, halves(total))
        found = lane_fold(total * coupled)
        rows.append(row_of(jnp.zeros_like(found), found))
        if tier < tiers - 1:
            row_out[tier] = rows[-1]
            start(q_copies(tier))
        return coupled

    for stage in range(stages - 1):
        for tier in reversed(range(low, tiers)):
            if stage + 1 < len(plans[1][tier]):
                forward(1, tier, stage)
        if stage == 0:
            for tier in range(low):
                place(tier, halves(quadratic(tier, total_of(1, tier))))
            base[...] = sums[...] + spread_low(low)
    e_copy.wait_send()
    for tier in range(low, tiers):
        total = total_of(1, tier)
        place(tier, halves(total))
        quadratic(tier, total)
    image_ref[...] = base[...] + spread_high(low)
    wait_all(row_in, row_recv)
    row = jnp.sum(row_in[...], axis=0) + sum(rows)
    columns = jnp.broadcast_to(row, (row.shape[1], row.shape[1])).T
    step_ref[...] = columns[:cols] / columns[cols:]

    wait_all(t_in, t_send)
    wait_all(row_in, row_send)


def local(rhs_matrix, initial_guess, leaf_blocks, row_bases, couplings):
    tiers, rank, leaf = row_bases.shape
    cols = initial_guess.shape[1]
    half = leaf // 2
    padded = pl.cdiv(rank, LANES) * LANES
    plans = [[plan_of(turn, tier) for tier in range(tiers)] for turn in range(2)]
    first, low = [sum(len(plan) == 1 for plan in each) for each in plans]
    slots, counts = layout_of(plans)
    row_count = row_layout(tiers)[1]
    assert 2 * cols == LANES and leaf_blocks.shape == (half, leaf) and low < tiers
    assert 2**tiers == lax.axis_size("leaf") and lax.axis_size("rhs") == 2
    any_spec = pl.BlockSpec(memory_space=pl.ANY)
    vmem_spec = pl.BlockSpec(memory_space=pltpu.VMEM)
    vmem, dma = pltpu.VMEM, pltpu.SemaphoreType.DMA
    packed = pack_shape(cols, rank)
    guess = initial_guess.T
    residual, image, step, held = pl.pallas_call(
        kernel,
        out_shape=[
            vmem((cols, leaf), F32),
            vmem((cols, leaf), F32),
            vmem((cols, LANES), F32),
            vmem((cols, leaf), F32),
        ],
        in_specs=[any_spec] * 5,
        out_specs=[vmem_spec] * 4,
        scratch_shapes=[
            vmem((cols, leaf), F32),
            vmem((half, leaf), F32),
            vmem((half, half), F32),
            vmem((tiers, rank, leaf), F32),
            vmem((tiers, rank, rank), F32),
            vmem((half, leaf), BF16),
            vmem((half, leaf), BF16),
            vmem((half, half), BF16),
            vmem((half, half), BF16),
            vmem((tiers, padded, leaf), BF16),
            vmem((tiers, padded, leaf), BF16),
            vmem((tiers, padded, padded), BF16),
            vmem((tiers, padded, padded), BF16),
            vmem((tiers - first, padded, leaf), BF16),
            vmem((tiers - first, padded, leaf), BF16),
            vmem((cols, leaf), BF16),
            vmem((cols, leaf), BF16),
            vmem((cols, tiers * padded), BF16),
            vmem((cols, tiers * padded), BF16),
            vmem(((tiers - first) * padded, tiers * padded), BF16),
            vmem(((tiers - first) * padded, tiers * padded), BF16),
            vmem((cols, tiers * padded), F32),
            vmem((cols, leaf), F32),
            vmem((cols, leaf), F32),
            vmem((len(slots), *packed), F32),
            vmem((sum(counts), *packed), F32),
            vmem((tiers, 1, LANES), F32),
            vmem((row_count, 1, LANES), F32),
            dma((6,)),
            dma,
            dma,
            dma,
            dma((len(slots),)),
            dma,
            dma,
        ],
        compiler_params=pltpu.CompilerParams(collective_id=0, has_side_effects=True),
        name="cg_step",
    )(guess, rhs_matrix.T, leaf_blocks, row_bases, couplings)
    alpha = jnp.tile(step, (1, leaf // LANES))
    return (held + alpha * residual).T, (residual - alpha * image).T


def solution(mesh):
    return jax.shard_map(
        local,
        mesh=mesh,
        in_specs=(
            P("leaf", "rhs"),
            P("leaf", "rhs"),
            P(("leaf", "rhs"), None),
            P(None, None, "leaf"),
            P(),
        ),
        out_specs=(P("leaf", "rhs"), P("leaf", "rhs")),
        check_vma=False,
    )
```

```python
import functools

import jax
import jax.numpy as jnp
from jax import lax
from jax.experimental import pallas as pl
from jax.experimental.pallas import tpu as pltpu
from jax.sharding import PartitionSpec as P

MESH = pl.DeviceIdType.MESH
F32 = jnp.float32
BF16 = jnp.bfloat16
LANES = 128
DIRECT = 8
NN = (((1,), (0,)), ((), ()))
NT = (((1,), (1,)), ((), ()))


def halves(value):
    high = value.astype(BF16)
    return high, (value - high.astype(F32)).astype(BF16)


def dot3(left, right, dims):
    rows = left[0].shape[0]
    stacked = lax.dot_general(
        jnp.concatenate(left, axis=0), right[0], dims, preferred_element_type=F32
    )
    cross = lax.dot_general(left[0], right[1], dims, preferred_element_type=F32)
    return stacked[:rows] + (stacked[rows:] + cross)


def lane_fold(value):
    total = value[:, :LANES]
    for start in range(LANES, value.shape[1], LANES):
        total = total + value[:, start : start + LANES]
    return total


def masks_over(low, high):
    return [value << low for value in range(2 ** (high - low) - 1, 0, -1)]


def plan_of(turn, tier):
    if turn == 1 and 2 ** (tier + 1) <= DIRECT:
        return [masks_over(0, tier + 1)]
    return [masks_over(low, min(low + 2, tier + 1)) for low in range(0, tier + 1, 2)]


def layout_of(plans):
    slots, counts = {}, []
    for turn, each in enumerate(plans):
        start_slot = sum(counts)
        total = start_slot
        for tier, plan in enumerate(each):
            for stage, masks in enumerate(plan):
                slots[turn, tier, stage] = total
                total += len(masks)
        counts.append(total - start_slot)
    return slots, counts


def row_layout(tiers):
    places, total = [], 2**tiers - 1
    for tier in range(tiers - 1):
        places.append(total)
        total += 2 ** (tiers - 1 - tier) - 1
    return places, total


def flip(leaf_index, mask):
    bit = 1
    while bit <= mask:
        if mask & bit:
            leaf_index = leaf_index + bit * (1 - 2 * ((leaf_index // bit) % 2))
        bit *= 2
    return leaf_index


def pack_shape(cols, rank):
    padded = pl.cdiv(rank, LANES) * LANES
    spare = padded - rank
    if padded != LANES or not spare or rank % spare or cols * spare % (8 * LANES):
        return cols, padded
    return cols * rank // LANES, LANES


def pack(value, rank):
    cols, padded = value.shape
    keep = pack_shape(cols, rank)[0]
    if keep == cols:
        return value
    spare = padded - rank
    extra = value[keep:]
    moved = [
        pltpu.roll(extra, (rank - start) % padded, axis=1) for start in range(0, rank, spare)
    ]
    lane = lax.broadcasted_iota(jnp.int32, (keep, padded), 1)
    return jnp.where(lane < rank, value[:keep], jnp.concatenate(moved, axis=0))


def unpack(value, cols, rank):
    keep, padded = value.shape
    if keep == cols:
        return value
    spare = padded - rank
    count = cols - keep
    lane = lax.broadcasted_iota(jnp.int32, (count, padded), 1)
    extra = jnp.zeros((count, padded), F32)
    for index, start in enumerate(range(0, rank, spare)):
        part = pltpu.roll(
            value[index * count : (index + 1) * count], (start - rank) % padded, axis=1
        )
        extra = jnp.where((lane >= start) & (lane < start + spare), part, extra)
    lane = lax.broadcasted_iota(jnp.int32, (keep, padded), 1)
    return jnp.concatenate([jnp.where(lane < rank, value, 0.0), extra], axis=0)


def row_of(upper, lower):
    stacked = jnp.concatenate([upper, lower], axis=0)
    return jnp.sum(stacked.T, axis=0, keepdims=True)


def kernel(
    x_hbm, b_hbm, d_hbm, u_hbm, c_hbm,
    r_ref, image_ref, step_ref, x_v,
    b_v, d_v, e_v, u_v, c_v,
    d_hi, d_lo, e_hi, e_lo, u_hi, u_lo, c_hi, c_lo, w_hi, w_lo, v_hi, v_lo, cc_hi, cc_lo,
    m_hi, m_lo, early, sums, base, t_out, t_in, row_out, row_in,
    local_sem, e_send, e_recv, t_send, t_recv, row_send, row_recv,
):
    tiers, rank, leaf = u_v.shape
    cols = x_v.shape[0]
    half = leaf // 2
    padded = u_hi.shape[1]
    me, core = lax.axis_index("leaf"), lax.axis_index("rhs")
    other = 1 - core
    mine = pl.ds(pl.multiple_of(core * half, half), half)
    theirs = pl.ds(pl.multiple_of(other * half, half), half)
    plans = [[plan_of(turn, tier) for tier in range(tiers)] for turn in range(2)]
    first, low = [sum(len(plan) == 1 for plan in each) for each in plans]
    everyone = masks_over(0, tiers)
    slots, counts = layout_of(plans)
    gates = {key: index for index, key in enumerate(slots)}
    places, _ = row_layout(tiers)
    near = [mask for masks in plans[0][-1] for mask in reversed(masks)]

    barrier = pltpu.get_barrier_semaphore()
    for target in [(flip(me, mask), core) for mask in near] + [(me, other)]:
        pl.semaphore_signal(barrier, inc=1, device_id=target, device_id_type=MESH)

    arrays = [(x_hbm, x_v)]
    arrays += [(u_hbm.at[part], u_v.at[part]) for part in (slice(tiers - 1, tiers), slice(0, tiers - 1))]
    arrays += [(d_hbm, d_v), (c_hbm, c_v), (b_hbm, b_v)]
    loads = [
        pltpu.make_async_copy(source, target, local_sem.at[index])
        for index, (source, target) in enumerate(arrays)
    ]
    for load in loads:
        load.start()
    x_load, *u_loads, d_load, c_load, b_load = loads

    def remote(source, target, send, recv, device):
        return pltpu.make_async_remote_copy(
            src_ref=source, dst_ref=target, send_sem=send, recv_sem=recv,
            device_id=device, device_id_type=MESH,
        )

    e_copy = remote(d_hbm.at[:, mine], e_v, e_send, e_recv, (me, other))

    def t_copies(turn, tier, stage):
        key = (turn, tier, stage)
        return [
            remote(
                t_out.at[gates[key]], t_in.at[slots[key] + index],
                t_send, t_recv.at[gates[key]], (flip(me, mask), core),
            )
            for index, mask in enumerate(plans[turn][tier][stage])
        ]

    def s_copies():
        return [
            remote(row_out.at[tiers - 1], row_in.at[index], row_send, row_recv, (flip(me, mask), core))
            for index, mask in enumerate(everyone)
        ]

    def q_copies(tier):
        return [
            remote(
                row_out.at[tier], row_in.at[places[tier] + index], row_send, row_recv,
                (flip(me, mask), core),
            )
            for index, mask in enumerate(masks_over(tier + 1, tiers))
        ]

    def start(copies):
        for copy in copies:
            copy.start()

    def wait_all(buffer, sem):
        pltpu.make_async_copy(buffer, buffer, sem).wait()

    if padded > rank:
        blank = jnp.zeros((tiers, padded - rank, leaf), BF16)
        u_hi[:, rank:, :] = blank
        u_lo[:, rank:, :] = blank
    c_hi[...] = jnp.zeros_like(c_hi)
    c_lo[...] = jnp.zeros_like(c_lo)

    def project(turn, tier):
        products = dot3((v_hi[...], v_lo[...]), (u_hi[tier], u_lo[tier]), NT)
        t_out[gates[turn, tier, 0]] = pack(products, rank)

    def gathered(turn, tier, stage):
        key = (turn, tier, stage)
        into = t_in.at[slots[key] : slots[key] + len(plans[turn][tier][stage])]
        wait_all(into, t_recv.at[gates[key]])
        return t_out[gates[key]] + jnp.sum(into[...], axis=0)

    def forward(turn, tier, stage):
        t_out[gates[turn, tier, stage + 1]] = gathered(turn, tier, stage)
        start(t_copies(turn, tier, stage + 1))

    def total_of(turn, tier):
        return unpack(gathered(turn, tier, len(plans[turn][tier]) - 1), cols, rank)

    def couple(tier, total):
        return dot3(total, (c_hi[tier], c_lo[tier]), NT)

    def place(tier, value):
        at = slice(tier * padded, (tier + 1) * padded)
        cc_hi[:, at], cc_lo[:, at] = value

    def spread(first, last, parts):
        at = slice(first * padded, last * padded)
        count = (last - first) * padded
        return dot3(
            (cc_hi[:, at], cc_lo[:, at]),
            tuple(part.reshape(count, leaf) for part in parts),
            NN,
        )

    def spread_low(last):
        return spread(0, last, (u_hi[:last], u_lo[:last]))

    def spread_high(start_tier):
        return spread(
            start_tier, tiers, (w_hi[start_tier - first :], w_lo[start_tier - first :])
        )

    def dense_own():
        sums[:, mine] = dot3((v_hi[...], v_lo[...]), (d_hi[...], d_lo[...]), NT)
        sums[:, theirs] = dot3(
            (v_hi[:, mine], v_lo[:, mine]), (d_hi[:, theirs], d_lo[:, theirs]), NN
        )

    def dense_rest():
        sums[:, theirs] = sums[:, theirs] + dot3(
            (v_hi[:, theirs], v_lo[:, theirs]), (e_hi[...], e_lo[...]), NN
        )

    stages = len(plans[0][-1])

    x_load.wait()
    v_hi[...], v_lo[...] = halves(x_v[...])
    for index, tier in enumerate(reversed(range(tiers))):
        if index < 2:
            u_loads[index].wait()
        u_hi[tier, :rank], u_lo[tier, :rank] = halves(u_v[tier])
        project(0, tier)
        if index == 0:
            pl.semaphore_wait(barrier, len(near) + 1)
        start(t_copies(0, tier, 0))
        if index == 0:
            e_copy.start()
    d_load.wait()
    d_hi[...], d_lo[...] = halves(d_v[...])
    dense_own()
    c_load.wait()
    c_hi[:, :rank, :rank], c_lo[:, :rank, :rank] = halves(c_v[...])
    for tier in range(first, tiers):
        w_hi[tier - first], w_lo[tier - first] = halves(
            dot3((c_hi[tier], c_lo[tier]), (u_hi[tier], u_lo[tier]), NN)
        )
    every = tuple(part[...].reshape(tiers * padded, leaf) for part in (u_hi, u_lo))
    for stage in range(stages - 1):
        for tier in reversed(range(first, tiers)):
            if stage + 1 < len(plans[0][tier]):
                forward(0, tier, stage)
            if stage == 0 and tier == tiers - 1:
                e_copy.wait_recv()
                e_hi[...], e_lo[...] = halves(e_v[...])
                dense_rest()
                b_load.wait()
                base[...] = b_v[...] - sums[...]
        if stage == 0:
            for tier in range(first):
                place(tier, halves(couple(tier, halves(total_of(0, tier)))))
            base[...] = base[...] - spread_low(first)
            early[...] = dot3(halves(base[...]), every, NT)
            count = (tiers - first) * padded
            spreads = tuple(part[...].reshape(count, leaf) for part in (w_hi, w_lo))
            m_hi[...], m_lo[...] = halves(dot3(spreads, every, NT))
    inner = (low - first) * padded
    if inner:
        for tier in range(first, low):
            place(tier, halves(total_of(0, tier)))
        at = slice(first * padded, low * padded)
        early[...] = early[...] - dot3(
            (cc_hi[:, at], cc_lo[:, at]), (m_hi[:inner], m_lo[:inner]), NN
        )
        base[...] = base[...] - spread(first, low, (w_hi[: low - first], w_lo[: low - first]))
    for tier in range(low, tiers):
        place(tier, halves(total_of(0, tier)))
    late = slice(low * padded, tiers * padded)
    products = early[...] - dot3(
        (cc_hi[:, late], cc_lo[:, late]), (m_hi[inner:], m_lo[inner:]), NN
    )
    for tier in [*reversed(range(low, tiers)), *range(low)]:
        t_out[gates[1, tier, 0]] = pack(products[:, tier * padded : (tier + 1) * padded], rank)
        start(t_copies(1, tier, 0))
    residual = base[...] - spread_high(low)
    r_ref[...] = residual
    v_hi[...], v_lo[...] = halves(residual)
    dense_own()
    dense_rest()
    r_now = r_ref[...]
    rows = [row_of(lane_fold(r_now * r_now), lane_fold(r_now * sums[...]))]
    row_out[tiers - 1] = rows[0]
    start(s_copies())

    def quadratic(tier, total):
        coupled = couple(tier, halves(total))
        found = lane_fold(total * coupled)
        rows.append(row_of(jnp.zeros_like(found), found))
        if tier < tiers - 1:
            row_out[tier] = rows[-1]
            start(q_copies(tier))
        return coupled

    for stage in range(stages - 1):
        for tier in reversed(range(low, tiers)):
            if stage + 1 < len(plans[1][tier]):
                forward(1, tier, stage)
        if stage == 0:
            for tier in range(low):
                place(tier, halves(quadratic(tier, total_of(1, tier))))
            base[...] = sums[...] + spread_low(low)
    e_copy.wait_send()
    for tier in range(low, tiers):
        total = total_of(1, tier)
        place(tier, halves(total))
        quadratic(tier, total)
    image_ref[...] = base[...] + spread_high(low)
    wait_all(row_in, row_recv)
    row = jnp.sum(row_in[...], axis=0) + sum(rows)
    columns = jnp.broadcast_to(row, (row.shape[1], row.shape[1])).T
    step_ref[...] = columns[:cols] / columns[cols:]

    wait_all(t_in, t_send)
    wait_all(row_in, row_send)


def local(rhs_matrix, initial_guess, leaf_blocks, row_bases, couplings):
    tiers, rank, leaf = row_bases.shape
    cols = initial_guess.shape[1]
    half = leaf // 2
    padded = pl.cdiv(rank, LANES) * LANES
    plans = [[plan_of(turn, tier) for tier in range(tiers)] for turn in range(2)]
    first, low = [sum(len(plan) == 1 for plan in each) for each in plans]
    slots, counts = layout_of(plans)
    row_count = row_layout(tiers)[1]
    assert 2 * cols == LANES and leaf_blocks.shape == (half, leaf) and low < tiers
    assert 2**tiers == lax.axis_size("leaf") and lax.axis_size("rhs") == 2
    any_spec = pl.BlockSpec(memory_space=pl.ANY)
    vmem_spec = pl.BlockSpec(memory_space=pltpu.VMEM)
    vmem, dma = pltpu.VMEM, pltpu.SemaphoreType.DMA
    packed = pack_shape(cols, rank)
    guess = initial_guess.T
    residual, image, step, held = pl.pallas_call(
        kernel,
        out_shape=[
            vmem((cols, leaf), F32),
            vmem((cols, leaf), F32),
            vmem((cols, LANES), F32),
            vmem((cols, leaf), F32),
        ],
        in_specs=[any_spec] * 5,
        out_specs=[vmem_spec] * 4,
        scratch_shapes=[
            vmem((cols, leaf), F32),
            vmem((half, leaf), F32),
            vmem((half, half), F32),
            vmem((tiers, rank, leaf), F32),
            vmem((tiers, rank, rank), F32),
            vmem((half, leaf), BF16),
            vmem((half, leaf), BF16),
            vmem((half, half), BF16),
            vmem((half, half), BF16),
            vmem((tiers, padded, leaf), BF16),
            vmem((tiers, padded, leaf), BF16),
            vmem((tiers, padded, padded), BF16),
            vmem((tiers, padded, padded), BF16),
            vmem((tiers - first, padded, leaf), BF16),
            vmem((tiers - first, padded, leaf), BF16),
            vmem((cols, leaf), BF16),
            vmem((cols, leaf), BF16),
            vmem((cols, tiers * padded), BF16),
            vmem((cols, tiers * padded), BF16),
            vmem(((tiers - first) * padded, tiers * padded), BF16),
            vmem(((tiers - first) * padded, tiers * padded), BF16),
            vmem((cols, tiers * padded), F32),
            vmem((cols, leaf), F32),
            vmem((cols, leaf), F32),
            vmem((len(slots), *packed), F32),
            vmem((sum(counts), *packed), F32),
            vmem((tiers, 1, LANES), F32),
            vmem((row_count, 1, LANES), F32),
            dma((6,)),
            dma,
            dma,
            dma,
            dma((len(slots),)),
            dma,
            dma,
        ],
        compiler_params=pltpu.CompilerParams(collective_id=0, has_side_effects=True),
        name="cg_step",
    )(guess, rhs_matrix.T, leaf_blocks, row_bases, couplings)
    alpha = jnp.tile(step, (1, leaf // LANES))
    return (held + alpha * residual).T, (residual - alpha * image).T


def solution(mesh):
    return jax.shard_map(
        local,
        mesh=mesh,
        in_specs=(
            P("leaf", "rhs"),
            P("leaf", "rhs"),
            P(("leaf", "rhs"), None),
            P(None, None, "leaf"),
            P(),
        ),
        out_specs=(P("leaf", "rhs"), P("leaf", "rhs")),
        check_vma=False,
    )
```
